32 devices in a mesh: kv: 4 (over y, x), seq: 8 (over z, core).
Axes of the slice: x: 2, y: 2, z: 4, core: 2. Of those that a mesh axis runs over, the one named last changes fastest.
Arguments:
- sampled_rows: int32 [768], replicated, may hold values from 0 to 2047, as said below
- query_vectors: bfloat16 [768, 64, 128], P('seq', 'kv'), may hold values from -150 to 150
- key_vectors: bfloat16 [2048, 8, 128], P('seq', 'kv'), may hold values from -6 to 6
Outputs:
- heavy_hitters: float32 [2048], P('seq')
The draws below stay inside these ranges and needn't reach their ends.
Inputs may be any that keep to these rules, and one draw needn't show every extreme that they name: `sampled_rows`: strictly increasing sequence positions.
All inputs are finite; a program needn't handle non-finite values.
Results may differ from the reference program's by a relative error of at most 0.0003.
Values may be sent and summed in bfloat16 or wider, within the bound.
No kernel may reach another device: no remote copies, remote signals or barrier semaphores. Data moves between devices by JAX's collectives and lax.ppermute only.
A program may use at most 64 MiB of HBM per device.

```python
import math
import jax
import jax.numpy as jnp
from jax import lax

KVH = 8
HEADS = 64
HD = 128
KEYS = 2048
ROWS = 768


def joint_draw(key):
    row_seed = jax.random.fold_in(key, 101)
    key_seed = jax.random.fold_in(key, 202)
    query_seed = jax.random.fold_in(key, 303)
    rows = jnp.sort(jax.random.permutation(row_seed, KEYS)[:ROWS]).astype(jnp.int32)
    vectors = jax.random.truncated_normal(key_seed, -6.0, 6.0, (KEYS, KVH, HD), jnp.float32)
    queries = jax.random.truncated_normal(query_seed, -6.0, 6.0, (ROWS, HEADS, HD), jnp.float32)
    return (rows, queries, vectors)


def draw_sampled_rows(key, part):
    return joint_draw(key)[0]


def draw_query_vectors(key, part):
    return joint_draw(key)[1].astype(jnp.bfloat16)


def draw_key_vectors(key, part):
    return joint_draw(key)[2].astype(jnp.bfloat16)


def setup_inputs(seed: int = 0) -> dict:
    keys = jax.random.split(jax.random.key(seed), 4)
    sampled_rows = draw_sampled_rows(jax.random.fold_in(keys[3], 71), 0)
    query_vectors = draw_query_vectors(jax.random.fold_in(keys[3], 71), 0)
    key_vectors = draw_key_vectors(jax.random.fold_in(keys[3], 71), 0)
    return dict(sampled_rows=sampled_rows, query_vectors=query_vectors, key_vectors=key_vectors)


NEG = -1e+30

def block_scores(query_block, key_block, factor):
    return jnp.einsum('rgid,kgd->rgik', query_block.astype(jnp.float32), key_block.astype(jnp.float32), precision=lax.Precision.HIGHEST) * factor

def visibility(rows_block, offset, amount):
    places = offset + jnp.arange(amount, dtype=jnp.int32)
    return places[None, None, None, :] <= rows_block[:, None, None, None]

def stats_block(query_block, rows_block, key_block, offset, running, factor):
    row_max, row_total = running
    scores = block_scores(query_block, key_block, factor)
    visible = visibility(rows_block, offset, key_block.shape[0])
    scores = jnp.where(visible, scores, NEG)
    new_max = jnp.maximum(row_max, lax.optimization_barrier(jnp.max(scores, axis=-1)))
    terms = jnp.where(visible, jnp.exp(scores - new_max[..., None]), 0.0)
    return (new_max, row_total * jnp.exp(row_max - new_max) + lax.optimization_barrier(jnp.sum(terms, axis=-1)))

def prob_columns(query_block, rows_block, key_block, offset, log_total, factor):
    scores = block_scores(query_block, key_block, factor)
    visible = visibility(rows_block, offset, key_block.shape[0])
    probability = jnp.where(visible, jnp.exp(scores - log_total[..., None]), 0.0)
    return lax.optimization_barrier(jnp.sum(probability, axis=(0, 1, 2)))

def reference(sampled_rows, query_vectors, key_vectors):
    total_rows = sampled_rows.shape[0]
    total_keys = key_vectors.shape[0]
    group_size = HEADS // KVH
    grouped = query_vectors.reshape(total_rows, KVH, group_size, HD)
    factor = 1.0 / math.sqrt(HD)
    row_stride = math.gcd(total_rows, 256)
    key_stride = math.gcd(total_keys, 1024)
    key_steps = jnp.arange(total_keys // key_stride, dtype=jnp.int32)

    def row_step(heaviness, row_index):
        first = row_index * row_stride
        query_block = lax.dynamic_slice_in_dim(grouped, first, row_stride, 0)
        rows_block = lax.dynamic_slice_in_dim(sampled_rows, first, row_stride, 0)
        highest = jnp.max(rows_block)

        def sweep(running, key_index):
            offset = key_index * key_stride

            def active(state):
                key_block = lax.dynamic_slice_in_dim(key_vectors, offset, key_stride, 0)
                return stats_block(query_block, rows_block, key_block, offset, state, factor)
            return (lax.cond(offset <= highest, active, lambda state: state, running), None)
        initial = (jnp.full((row_stride, KVH, group_size), NEG, jnp.float32), jnp.zeros((row_stride, KVH, group_size), jnp.float32))
        (row_max, row_total), _ = lax.scan(sweep, initial, key_steps)
        log_total = row_max + jnp.log(row_total)

        def spread(acc, key_index):
            offset = key_index * key_stride

            def active(state):
                key_block = lax.dynamic_slice_in_dim(key_vectors, offset, key_stride, 0)
                column = prob_columns(query_block, rows_block, key_block, offset, log_total, factor)
                return lax.dynamic_update_slice_in_dim(state, lax.dynamic_slice_in_dim(state, offset, key_stride, 0) + column, offset, 0)
            return (lax.cond(offset <= highest, active, lambda state: state, acc), None)
        heaviness, _ = lax.scan(spread, heaviness, key_steps)
        return (heaviness, None)
    heaviness, _ = lax.scan(row_step, jnp.zeros((total_keys,), jnp.float32), jnp.arange(total_rows // row_stride, dtype=jnp.int32))
    return heaviness * (1.0 / group_size)
```

```python
import math

import jax
import jax.numpy as jnp
from jax import lax
from jax.sharding import PartitionSpec as P

NEG = -1e30


def block_scores(query_block, key_block, factor):
    return (
        jnp.einsum("rgid,kgd->rgik", query_block, key_block, preferred_element_type=jnp.float32)
        * factor
    )


def gather_keys(key_vectors):
    size = lax.axis_size("seq")
    if size & (size - 1) or size > 16:
        return lax.all_gather(key_vectors, "seq", axis=0, tiled=True)
    me = lax.axis_index("seq")
    swap = [(i, i ^ 1) for i in range(size)]
    slots = {0: key_vectors}
    far = sorted(range(2, size, 2), key=lambda j: (j & (j - 1) != 0, -j))
    for j in far:
        slots[j] = lax.ppermute(key_vectors, "seq", [(i, i ^ j) for i in range(size)])
    for j in range(0, size, 2):
        slots[j + 1] = lax.ppermute(slots[j], "seq", swap)
    stacked = jnp.stack([slots[j] for j in range(size)])
    ordered = jnp.take(stacked, me ^ jnp.arange(size), axis=0)
    return ordered.reshape((size * key_vectors.shape[0],) + key_vectors.shape[1:])


def on_device(sampled_rows, query_vectors, key_vectors):
    local_rows, _, depth = query_vectors.shape
    local_keys, local_groups, _ = key_vectors.shape
    group_size = query_vectors.shape[1] // local_groups
    factor = 1.0 / math.sqrt(depth)
    size = lax.axis_size("seq")
    others = lax.axis_size("kv")
    grouped = query_vectors.reshape(local_rows, local_groups, group_size, depth)
    own_rows = lax.dynamic_slice_in_dim(
        sampled_rows, lax.axis_index("seq") * local_rows, local_rows, 0
    )
    gathered = gather_keys(key_vectors)
    places = jnp.arange(size * local_keys, dtype=jnp.int32)
    stride = math.gcd(size * local_keys, 2048)

    def visible(first):
        return (first + places[:stride])[None, None, None, :] <= own_rows[:, None, None, None]

    def keys_at(first):
        return lax.dynamic_slice_in_dim(gathered, first, stride, 0)

    def stats(running, first):
        row_max, row_total = running
        scores = jnp.where(visible(first), block_scores(grouped, keys_at(first), factor), NEG)
        new_max = jnp.maximum(row_max, jnp.max(scores, axis=-1))
        terms = jnp.where(visible(first), jnp.exp(scores - new_max[..., None]), 0.0)
        return (new_max, row_total * jnp.exp(row_max - new_max) + jnp.sum(terms, axis=-1)), None

    shape = (local_rows, local_groups, group_size)
    initial = (jnp.full(shape, NEG, jnp.float32), jnp.zeros(shape, jnp.float32))
    firsts = jnp.arange(size * local_keys // stride, dtype=jnp.int32) * stride
    (row_max, row_total), _ = lax.scan(stats, initial, firsts)
    log_total = row_max + jnp.log(row_total)

    def columns(first):
        scores = block_scores(grouped, keys_at(first), factor)
        terms = jnp.where(visible(first), jnp.exp(scores - log_total[..., None]), 0.0)
        return jnp.sum(terms, axis=(0, 1, 2))

    partial = lax.map(columns, firsts).reshape(1, size, local_keys)
    partial = jnp.broadcast_to(partial, (others, size, local_keys)).reshape(-1, local_keys)
    received = lax.all_to_all(partial, ("kv", "seq"), 0, 0, tiled=True)
    return jnp.sum(received, axis=0) * (1.0 / group_size)


def solution(mesh):
    placed = (P(), P("seq", "kv", None), P("seq", "kv", None))
    return jax.shard_map(on_device, mesh=mesh, in_specs=placed, out_specs=P("seq"), check_vma=False)
```

```python
import functools
import math

import jax
import jax.numpy as jnp
from jax import lax
from jax.experimental import pallas as pl
from jax.experimental.pallas import tpu as pltpu
from jax.sharding import PartitionSpec as P

NEG = -1e30
SPAN = 2048
LANES = 256


def column_kernel(counts, copies, offsets, pos_ref, query_ref, *refs):
    key_refs, (out_ref, keys, plain, queries, scores, total) = refs[: len(counts)], refs[len(counts) :]
    rows, heads, depth = query_ref.shape
    groups = keys.shape[0]
    size = heads // groups
    block = plain.shape[0] // groups
    amount = keys.shape[1]
    span = math.gcd(amount, SPAN)
    width = rows * size
    factor = math.log2(math.e) / math.sqrt(depth)

    def split(ref, index, first):
        plain[...] = ref[pl.ds(index * groups * block, groups * block), :].astype(jnp.float32)
        for g in range(groups):
            part = plain[pl.ds(g, block, stride=groups), :]
            keys[g, pl.ds(first, block), :] = part.astype(keys.dtype)

    done = 0
    for ref, count in zip(key_refs, counts, strict=True):
        if count == 1:
            split(ref, 0, done * block)
        else:

            @pl.loop(0, count)
            def _(i, ref=ref, done=done):
                split(ref, i, pl.multiple_of((done + i) * block, block))

        done += count
    wide = query_ref[...].astype(jnp.float32)
    for g in range(groups):
        part = wide[:, g * size : (g + 1) * size, :].reshape(width, depth)
        queries[g] = part.astype(queries.dtype)
    total[...] = jnp.zeros_like(total)
    places = lax.broadcasted_iota(jnp.int32, (block, LANES), 0)

    def over_spans(step, carry):
        if amount == span:
            return step(0, carry)
        return lax.fori_loop(
            0, amount // span, lambda i, c: step(pl.multiple_of(i * span, span), c), carry
        )

    tiles = width // LANES

    @pl.loop(0, groups * tiles)
    def _(step):
        g = step // tiles
        lanes = pl.ds(pl.multiple_of((step % tiles) * LANES, LANES), LANES)
        query = queries[g, lanes, :]
        position = pos_ref[:, lanes]

        def largest(first, top):
            for b in range(span // block):
                here = pl.ds(first + b * block, block)
                value = lax.dot_general(
                    keys[g, here, :], query, (((1,), (1,)), ((), ())),
                    preferred_element_type=jnp.float32,
                )
                limit = position - offsets[first // block + b]
                value = jnp.where(places <= limit, value, NEG)
                scores[here, :] = value
                top = jnp.maximum(top, jnp.max(value.reshape(block // 8, 8, LANES), axis=0))
            return top

        top = over_spans(largest, jnp.full((8, LANES), NEG, jnp.float32))
        top = jnp.max(top, axis=0, keepdims=True)

        def terms(first, summed):
            for b in range(span // block):
                here = pl.ds(first + b * block, block)
                value = jnp.exp2((scores[here, :] - top) * factor)
                scores[here, :] = value
                summed = summed + jnp.sum(value.reshape(block // 8, 8, LANES), axis=0)
            return summed

        summed = over_spans(terms, jnp.zeros((8, LANES), jnp.float32))
        weight = 1.0 / jnp.sum(summed, axis=0, keepdims=True)

        def spread(first, carry):
            for b in range(span // block):
                here = pl.ds(first + b * block, block)
                value = scores[here, :] * weight
                part = value[:, :128]
                for i in range(1, LANES // 128):
                    part = part + value[:, i * 128 : (i + 1) * 128]
                total[here, :] += part
            return carry

        over_spans(spread, 0)

    ones = jnp.ones((8, 128), jnp.float32)

    def finish(index):
        here = pl.ds(pl.multiple_of(index * block, block), block)
        line = lax.dot_general(
            ones, total[here, :], (((1,), (1,)), ((), ())),
            precision=lax.Precision.HIGHEST, preferred_element_type=jnp.float32,
        )[:1]
        row = offsets[index] // block
        for i in range(copies):
            out_ref[pl.ds(i * (amount // block) + row, 1), :] = line * (1.0 / size)

    if amount == span:
        for index in range(amount // block):
            finish(index)
    else:

        @pl.loop(0, amount // block)
        def _(index):
            finish(index)


def gather_keys(key_vectors):
    size = lax.axis_size("seq")
    me = lax.axis_index("seq")
    if size & (size - 1) or size > 16:
        return [lax.all_gather(key_vectors, "seq", axis=0, tiled=True)], [size], jnp.arange(size)
    swap = [(i, i ^ 1) for i in range(size)]
    slots = {0: key_vectors}
    far = sorted(range(2, size, 2), key=lambda j: (j & (j - 1) == 0, -j))
    if size == 8:
        far = [4, 6, 2]
    for j in far:
        slots[j] = lax.ppermute(key_vectors, "seq", [(i, i ^ j) for i in range(size)])
    for j in range(0, size, 2):
        slots[j + 1] = lax.ppermute(slots[j], "seq", swap)
    return [slots[j] for j in range(size)], [1] * size, me ^ jnp.arange(size)


def on_device(sampled_rows, query_vectors, key_vectors):
    local_rows, heads, depth = query_vectors.shape
    local_keys, groups, _ = key_vectors.shape
    size = heads // groups
    members = lax.axis_size("seq")
    others = lax.axis_size("kv")
    own_rows = lax.dynamic_slice_in_dim(
        sampled_rows, lax.axis_index("seq") * local_rows, local_rows, 0
    )
    position = jnp.repeat(own_rows, size)[None, :]
    blocks, counts, owner = gather_keys(key_vectors)
    blocks = [b.reshape(-1, depth) for b in blocks]
    amount = members * local_keys
    whole = pl.BlockSpec(memory_space=pltpu.VMEM)
    partial = pl.pallas_call(
        functools.partial(column_kernel, counts, others),
        out_shape=jax.ShapeDtypeStruct((others * members, local_keys), jnp.float32),
        in_specs=[pl.BlockSpec(memory_space=pltpu.SMEM)] + [whole] * (2 + len(blocks)),
        out_specs=whole,
        scratch_shapes=[
            pltpu.VMEM((groups, amount, depth), jnp.bfloat16),
            pltpu.VMEM((groups * local_keys, depth), jnp.float32),
            pltpu.VMEM((groups, local_rows * size, depth), jnp.bfloat16),
            pltpu.VMEM((amount, LANES), jnp.float32),
            pltpu.VMEM((amount, 128), jnp.float32),
        ],
        compiler_params=pltpu.CompilerParams(vmem_limit_bytes=60 << 20),
    )(owner.astype(jnp.int32) * local_keys, position, query_vectors, *blocks)
    received = lax.all_to_all(partial, ("kv", "seq"), 0, 0, tiled=True)
    return jnp.sum(received, axis=0)


def solution(mesh):
    placed = (P(), P("seq", "kv", None), P("seq", "kv", None))
    return jax.shard_map(on_device, mesh=mesh, in_specs=placed, out_specs=P("seq"), check_vma=False)
```

```python
import functools
import math

import jax
import jax.numpy as jnp
from jax import lax
from jax.experimental import pallas as pl
from jax.experimental.pallas import tpu as pltpu
from jax.sharding import PartitionSpec as P

NEG = -1e30
SPAN = 2048
LANES = 256
CHUNK = 256
CONTRACT_LAST = (((1,), (1,)), ((), ()))
CONTRACT_INNER = (((1,), (0,)), ((), ()))
WHOLE = pl.BlockSpec(memory_space=pltpu.VMEM)
SCALARS = pl.BlockSpec(memory_space=pltpu.SMEM)


def round_up(value, step):
    return -(-value // step) * step


def prepare_kernel(offsets, row_ref, query_ref, mask_ref, turned_ref):
    rows, heads, depth = query_ref.shape
    groups, _, width = turned_ref.shape
    size = heads // groups
    extra = mask_ref.shape[1]
    block = mask_ref.shape[0] // offsets.shape[0]
    column = lax.broadcasted_iota(jnp.int32, (block, extra), 1)
    place = lax.broadcasted_iota(jnp.int32, (block, extra), 0)
    position = row_ref[...]

    def mask(index):
        hidden = (place + offsets[index] > position) & (column < rows)
        value = jnp.where(hidden, NEG, 0.0)
        mask_ref[pl.ds(pl.multiple_of(index * block, block), block), :] = value.astype(mask_ref.dtype)

    pl.loop(0, offsets.shape[0])(mask)
    wide = query_ref[...].astype(jnp.float32)
    eye = (
        lax.broadcasted_iota(jnp.int32, (depth, depth), 0)
        == lax.broadcasted_iota(jnp.int32, (depth, depth), 1)
    )
    eye = jnp.where(eye, 1.0, 0.0).astype(jnp.bfloat16)
    owner = lax.broadcasted_iota(jnp.int32, (extra, width), 1) // size
    hot = owner == lax.broadcasted_iota(jnp.int32, (extra, width), 0)
    hot = jnp.where(hot, 1.0, 0.0).astype(jnp.bfloat16)
    for g in range(groups):
        part = wide[:, g * size : (g + 1) * size, :].reshape(width, depth).astype(jnp.bfloat16)
        turned = lax.dot_general(eye, part, CONTRACT_LAST, preferred_element_type=jnp.float32)
        turned_ref[g, :depth, :] = turned.astype(turned_ref.dtype)
        turned_ref[g, depth:, :] = hot


def column_kernel(counts, copies, rows, offsets, mask_ref, turned_ref, *refs):
    key_refs, (out_ref, keys, plain, total, *scores) = refs[: len(counts)], refs[len(counts) :]
    groups, amount, depth = keys.shape
    width = turned_ref.shape[2]
    block = plain.shape[0] // groups
    chunk = math.gcd(amount, CHUNK)
    factor = math.log2(math.e) / math.sqrt(depth)

    def split(ref, index, first):
        plain[...] = ref[pl.ds(index * groups * block, groups * block), :].astype(jnp.float32)
        for g in range(groups):
            part = plain[pl.ds(g, block, stride=groups), :]
            keys[g, pl.ds(first, block), :] = part.astype(keys.dtype)

    done = 0
    for ref, count in zip(key_refs, counts, strict=True):
        if count == 1:
            split(ref, 0, done * block)
        else:

            @pl.loop(0, count)
            def _(i, ref=ref, done=done):
                split(ref, i, pl.multiple_of((done + i) * block, block))

        done += count
    tiles = groups * (width // LANES)

    def lanes_of(step):
        first = (step % (width // LANES)) * LANES
        return step // (width // LANES), pl.ds(pl.multiple_of(first, LANES), LANES)

    def score(step, here, held, top):
        g, lanes = lanes_of(step)
        left = jnp.concatenate([keys[g, here, :], mask_ref[here, :]], axis=1)
        value = lax.dot_general(
            left, turned_ref[g, :, lanes], CONTRACT_INNER, preferred_element_type=jnp.float32
        )
        held[here, :] = value
        return jnp.maximum(top, jnp.max(value.reshape(chunk // 8, 8, LANES), axis=0))

    def term(here, held, top, summed):
        value = jnp.exp2((held[here, :] - top) * factor)
        held[here, :] = value
        return summed + jnp.sum(value.reshape(chunk // 8, 8, LANES), axis=0)

    def spread(here, held, weight, first):
        value = held[here, :] * weight
        part = value[:, :128]
        for i in range(1, LANES // 128):
            part = part + value[:, i * 128 : (i + 1) * 128]
        total[here, :] = part if first else total[here, :] + part

    lowest = jnp.full((8, LANES), NEG, jnp.float32)
    nothing = jnp.zeros((8, LANES), jnp.float32)
    if amount <= SPAN:
        top, weight = {}, {}
        for step in range(tiles + 2):
            high, summed = lowest, nothing
            for b in range(amount // chunk):
                here = pl.ds(b * chunk, chunk)
                if 0 <= step - 2:
                    spread(here, scores[(step - 2) % 3], weight[step - 2], step == 2)
                if 0 <= step - 1 < tiles:
                    summed = term(here, scores[(step - 1) % 3], top[step - 1], summed)
                if step < tiles:
                    high = score(step, here, scores[step % 3], high)
            if step < tiles:
                top[step] = jnp.max(high, axis=0, keepdims=True)
            if 0 <= step - 1 < tiles:
                weight[step - 1] = 1.0 / jnp.sum(summed, axis=0, keepdims=True)
    else:
        total[...] = jnp.zeros_like(total)

        def over(body, carry):
            def at(i, c):
                return body(pl.ds(pl.multiple_of(i * chunk, chunk), chunk), c)

            return lax.fori_loop(0, amount // chunk, at, carry)

        @pl.loop(0, tiles)
        def _(step):
            held = scores[0]
            high = over(lambda here, c: score(step, here, held, c), lowest)
            peak = jnp.max(high, axis=0, keepdims=True)
            summed = over(lambda here, c: term(here, held, peak, c), nothing)
            share = 1.0 / jnp.sum(summed, axis=0, keepdims=True)

            def last(here, c):
                spread(here, held, share, False)
                return c

            over(last, 0)

    ones = jnp.ones((16, 128), jnp.bfloat16)

    def finish(index):
        here = pl.ds(pl.multiple_of(index * block, block), block)
        high = total[here, :].astype(jnp.bfloat16)
        low = (total[here, :] - high.astype(jnp.float32)).astype(jnp.bfloat16)
        line = sum(
            lax.dot_general(ones, part, CONTRACT_LAST, preferred_element_type=jnp.float32)
            for part in (high, low)
        )[:1]
        row = offsets[index] // block
        line = line * (1.0 / (width // rows))
        for i in range(copies):
            out_ref[i * (amount // block) + row, :, :] = line

    if amount <= SPAN:
        for index in range(amount // block):
            finish(index)
    else:
        pl.loop(0, amount // block)(finish)


def gather_keys(key_vectors):
    size = lax.axis_size("seq")
    me = lax.axis_index("seq")
    if size & (size - 1) or size > 16:
        return [lax.all_gather(key_vectors, "seq", axis=0, tiled=True)], [size], jnp.arange(size)
    swap = [(i, i ^ 1) for i in range(size)]
    slots = {0: key_vectors}
    far = sorted(range(2, size, 2), key=lambda j: (j & (j - 1) == 0, -j))
    if size == 8:
        far = [4, 6, 2]
    for j in far:
        slots[j] = lax.ppermute(key_vectors, "seq", [(i, i ^ j) for i in range(size)])
    for j in range(0, size, 2):
        slots[j + 1] = lax.ppermute(slots[j], "seq", swap)
    return [slots[j] for j in range(size)], [1] * size, me ^ jnp.arange(size)


def on_device(sampled_rows, query_vectors, key_vectors):
    local_rows, heads, depth = query_vectors.shape
    local_keys, groups, _ = key_vectors.shape
    width = local_rows * heads // groups
    members = lax.axis_size("seq")
    others = lax.axis_size("kv")
    amount = members * local_keys
    extra = round_up(local_rows, 128)
    blocks, counts, owner = gather_keys(key_vectors)
    blocks = [b.reshape(-1, depth) for b in blocks]
    offsets = owner.astype(jnp.int32) * local_keys
    own_rows = lax.dynamic_slice_in_dim(
        sampled_rows, lax.axis_index("seq") * local_rows, local_rows, 0
    )
    own_rows = jnp.pad(own_rows, (0, extra - local_rows))[None, :]
    mask, turned = pl.pallas_call(
        prepare_kernel,
        out_shape=(
            jax.ShapeDtypeStruct((amount, extra), jnp.bfloat16),
            jax.ShapeDtypeStruct((groups, depth + extra, width), jnp.bfloat16),
        ),
        in_specs=[SCALARS, WHOLE, WHOLE],
        out_specs=(WHOLE, WHOLE),
        cost_estimate=pl.CostEstimate(flops=10**9, bytes_accessed=10**6, transcendentals=0),
        name="prepare",
    )(offsets, own_rows, query_vectors)
    partial = pl.pallas_call(
        functools.partial(column_kernel, counts, others, local_rows),
        out_shape=jax.ShapeDtypeStruct((others * members, 1, local_keys), jnp.float32),
        in_specs=[SCALARS] + [WHOLE] * (2 + len(blocks)),
        out_specs=WHOLE,
        scratch_shapes=[
            pltpu.VMEM((groups, amount, depth), jnp.bfloat16),
            pltpu.VMEM((groups * local_keys, depth), jnp.float32),
            pltpu.VMEM((amount, 128), jnp.float32),
        ]
        + [pltpu.VMEM((amount, LANES), jnp.float32)] * (3 if amount <= SPAN else 1),
        compiler_params=pltpu.CompilerParams(vmem_limit_bytes=(24 if amount <= 4096 else 60) << 20),
        name="columns",
    )(offsets, mask, turned, *blocks)
    received = lax.all_to_all(partial, ("kv", "seq"), 0, 0, tiled=True)
    return jnp.sum(received, axis=(0, 1))


def solution(mesh):
    placed = (P(), P("seq", "kv", None), P("seq", "kv", None))
    return jax.shard_map(on_device, mesh=mesh, in_specs=placed, out_specs=P("seq"), check_vma=False)
```

```python
import functools
import math

import jax
import jax.numpy as jnp
from jax import lax
from jax.experimental import pallas as pl
from jax.experimental.pallas import tpu as pltpu
from jax.sharding import PartitionSpec as P


NEG = -1e30
LOW = -1e20
SPAN = 2048
LANES = 256
CHUNK = 256
CONTRACT_LAST = (((1,), (1,)), ((), ()))
CONTRACT_INNER = (((1,), (0,)), ((), ()))
WHOLE = pl.BlockSpec(memory_space=pltpu.VMEM)
SCALARS = pl.BlockSpec(memory_space=pltpu.SMEM)


def grant(mebibytes):
    return pltpu.CompilerParams(vmem_limit_bytes=mebibytes << 20)


def round_up(value, step):
    return -(-value // step) * step


def prepare_kernel(offsets, row_ref, query_ref, mask_ref, turned_ref):
    rows, heads, depth = query_ref.shape
    groups, _, width = turned_ref.shape
    size = heads // groups
    extra = mask_ref.shape[1]
    block = mask_ref.shape[0] // offsets.shape[0]
    column = lax.broadcasted_iota(jnp.int32, (block, extra), 1)
    place = lax.broadcasted_iota(jnp.int32, (block, extra), 0)
    position = row_ref[...]

    def mask(index):
        hidden = (place + offsets[index] > position) & (column < rows)
        value = jnp.where(hidden, NEG, 0.0)
        mask_ref[pl.ds(pl.multiple_of(index * block, block), block), :] = value.astype(mask_ref.dtype)

    pl.loop(0, offsets.shape[0])(mask)
    wide = query_ref[...].astype(jnp.float32)
    eye = (
        lax.broadcasted_iota(jnp.int32, (depth, depth), 0)
        == lax.broadcasted_iota(jnp.int32, (depth, depth), 1)
    )
    eye = jnp.where(eye, 1.0, 0.0).astype(jnp.bfloat16)
    owner = lax.broadcasted_iota(jnp.int32, (extra, width), 1) // size
    hot = owner == lax.broadcasted_iota(jnp.int32, (extra, width), 0)
    hot = jnp.where(hot, 1.0, 0.0).astype(jnp.bfloat16)
    for g in range(groups):
        part = wide[:, g * size : (g + 1) * size, :].reshape(width, depth).astype(jnp.bfloat16)
        turned = lax.dot_general(eye, part, CONTRACT_LAST, preferred_element_type=jnp.float32)
        turned_ref[g, :depth, :] = turned.astype(turned_ref.dtype)
        turned_ref[g, depth:, :] = hot


def split_keys(key_refs, counts, keys, plain):
    groups = keys.shape[0]
    block = plain.shape[0] // groups

    def split(ref, index, first):
        plain[...] = ref[pl.ds(index * groups * block, groups * block), :].astype(jnp.float32)
        for g in range(groups):
            part = plain[pl.ds(g, block, stride=groups), :]
            keys[g, pl.ds(first, block), :] = part.astype(keys.dtype)

    done = 0
    for ref, count in zip(key_refs, counts, strict=True):
        if count == 1:
            split(ref, 0, done * block)
        else:

            @pl.loop(0, count)
            def _(i, ref=ref, done=done):
                split(ref, i, pl.multiple_of((done + i) * block, block))

        done += count


def tile_of(step, width):
    across = width // LANES
    first = (step % across) * LANES
    return step // across, pl.ds(pl.multiple_of(first, LANES), LANES)


def raw_scores(keys, mask_ref, turned_ref, step, here, base, held, top):
    g, lanes = tile_of(step, turned_ref.shape[2])
    shown = pl.ds(here.start + base, here.size)
    left = jnp.concatenate([keys[g, here, :], mask_ref[shown, :]], axis=1)
    value = lax.dot_general(
        left, turned_ref[g, :, lanes], CONTRACT_INNER, preferred_element_type=jnp.float32
    )
    held[here, :] = value
    return jnp.maximum(top, jnp.max(value.reshape(here.size // 8, 8, LANES), axis=0))


def stage_kernel(base, mask_ref, turned_ref, *refs):
    *key_refs, term_ref, top_ref, sum_ref, keys, plain, held = refs
    amount, depth = keys.shape[1:]
    width = turned_ref.shape[2]
    chunk = math.gcd(amount, CHUNK)
    factor = math.log2(math.e) / math.sqrt(depth)
    split_keys(key_refs, [1] * len(key_refs), keys, plain)

    @pl.loop(0, keys.shape[0] * (width // LANES))
    def _(step):
        columns = pl.ds(pl.multiple_of(step * LANES, LANES), LANES)
        top = jnp.full((8, LANES), LOW, jnp.float32)
        for b in range(amount // chunk):
            here = pl.ds(b * chunk, chunk)
            top = raw_scores(keys, mask_ref, turned_ref, step, here, base, held, top)
        top = jnp.max(top, axis=0, keepdims=True)
        summed = jnp.zeros((8, LANES), jnp.float32)
        for b in range(amount // chunk):
            here = pl.ds(b * chunk, chunk)
            value = jnp.exp2((held[here, :] - top) * factor)
            term_ref[here, columns] = value
            summed = summed + jnp.sum(value.reshape(chunk // 8, 8, LANES), axis=0)
        top_ref[:, columns] = top
        sum_ref[:, columns] = jnp.sum(summed, axis=0, keepdims=True)


def column_kernel(counts, copies, rows, early, offsets, mask_ref, turned_ref, *refs):
    stages = [refs[3 * i : 3 * i + 3] for i in range(early)]
    refs = refs[3 * early :]
    key_refs, (out_ref, keys, plain, total, *scores) = refs[: len(counts)], refs[len(counts) :]
    groups, amount, depth = keys.shape
    width = turned_ref.shape[2]
    block = plain.shape[0] // groups
    chunk = math.gcd(amount, CHUNK)
    factor = math.log2(math.e) / math.sqrt(depth)
    every = total.shape[0]
    base = every - amount
    split_keys(key_refs, counts, keys, plain)
    tiles = groups * (width // LANES)

    def score(step, here, held, top):
        return raw_scores(keys, mask_ref, turned_ref, step, here, base, held, top)

    def term(here, held, top, summed):
        value = jnp.exp2((held[here, :] - top) * factor)
        held[here, :] = value
        return summed + jnp.sum(value.reshape(here.size // 8, 8, LANES), axis=0)

    def spread(value, weight, there, first):
        value = value * weight
        part = value[:, :128]
        for i in range(1, LANES // 128):
            part = part + value[:, i * 128 : (i + 1) * 128]
        total[there, :] = part if first else total[there, :] + part

    lowest = jnp.full((8, LANES), LOW, jnp.float32)
    nothing = jnp.zeros((8, LANES), jnp.float32)
    if amount <= SPAN:
        top, weights = {}, {}
        parts = amount // chunk
        for step in range(tiles + 2):
            high, summed = lowest, nothing
            old = step - 2
            for b in range(parts):
                here = pl.ds(b * chunk, chunk)
                if 0 <= old:
                    first = 0
                    columns = pl.ds(old * LANES, LANES)
                    for (terms, _, _), weight in zip(stages, weights[old][1:], strict=True):
                        size = terms.shape[0] // parts
                        value = terms[pl.ds(b * size, size), columns]
                        spread(value, weight, pl.ds(first + b * size, size), old == 0)
                        first += terms.shape[0]
                    value = scores[old % 3][here, :]
                    spread(value, weights[old][0], pl.ds(base + b * chunk, chunk), old == 0)
                if 0 <= step - 1 < tiles:
                    summed = term(here, scores[(step - 1) % 3], top[step - 1], summed)
                if step < tiles:
                    high = score(step, here, scores[step % 3], high)
            if 0 <= step - 1 < tiles:
                columns = pl.ds((step - 1) * LANES, LANES)
                whole = jnp.sum(summed, axis=0, keepdims=True)
                scale = [jnp.exp2((s[1][:, columns] - top[step - 1]) * factor) for s in stages]
                for s, by in zip(stages, scale, strict=True):
                    whole = whole + s[2][:, columns] * by
                share = 1.0 / whole
                weights[step - 1] = [share] + [share * by for by in scale]
            if step < tiles:
                columns = pl.ds(step * LANES, LANES)
                peak = jnp.max(high, axis=0, keepdims=True)
                for s in stages:
                    peak = jnp.maximum(peak, s[1][:, columns])
                top[step] = peak
    else:
        total[...] = jnp.zeros_like(total)

        def over(body, carry):
            def at(i, c):
                return body(pl.ds(pl.multiple_of(i * chunk, chunk), chunk), c)

            return lax.fori_loop(0, amount // chunk, at, carry)

        @pl.loop(0, tiles)
        def _(step):
            held = scores[0]
            high = over(lambda here, c: score(step, here, held, c), lowest)
            peak = jnp.max(high, axis=0, keepdims=True)
            summed = over(lambda here, c: term(here, held, peak, c), nothing)
            share = 1.0 / jnp.sum(summed, axis=0, keepdims=True)

            def last(here, c):
                spread(held[here, :], share, here, False)
                return c

            over(last, 0)

    ones = jnp.ones((16, 128), jnp.bfloat16)

    def finish(index):
        here = pl.ds(pl.multiple_of(index * block, block), block)
        high = total[here, :].astype(jnp.bfloat16)
        low = (total[here, :] - high.astype(jnp.float32)).astype(jnp.bfloat16)
        line = sum(
            lax.dot_general(ones, part, CONTRACT_LAST, preferred_element_type=jnp.float32)
            for part in (high, low)
        )[:1]
        row = offsets[index] // block
        line = line * (1.0 / (width // rows))
        for i in range(copies):
            out_ref[i * (every // block) + row, :, :] = line

    if amount <= SPAN:
        for index in range(every // block):
            finish(index)
    else:
        pl.loop(0, every // block)(finish)


def gather_keys(key_vectors):
    size = lax.axis_size("seq")
    swap = [(i, i ^ 1) for i in range(size)]
    slots = {0: key_vectors}
    far = [4, 6, 2] if size == 8 else list(range(2, size, 2))
    for j in far:
        slots[j] = lax.ppermute(key_vectors, "seq", [(i, i ^ j) for i in range(size)])
    for j in [0] + far:
        slots[j + 1] = lax.ppermute(slots[j], "seq", swap)
    return slots, [i for j in [0] + far for i in (j, j + 1)]


def on_device(sampled_rows, query_vectors, key_vectors):
    local_rows, heads, depth = query_vectors.shape
    local_keys, groups, _ = key_vectors.shape
    width = local_rows * heads // groups
    members = lax.axis_size("seq")
    others = lax.axis_size("kv")
    me = lax.axis_index("seq")
    amount = members * local_keys
    extra = round_up(local_rows, 128)
    direct = members & (members - 1) == 0 and 2 < members <= 8
    if direct:
        slots, order = gather_keys(key_vectors)
        early = [order[i : i + 2] for i in range(0, members - 4, 2)]
        blocks = [slots[j] for j in order]
        counts = [1] * 4
        owner = me ^ jnp.array(order, jnp.int32)
    else:
        early = []
        blocks = [lax.all_gather(key_vectors, "seq", axis=0, tiled=True)]
        counts = [members]
        owner = jnp.arange(members, dtype=jnp.int32)
    blocks = [b.reshape(-1, depth) for b in blocks]
    offsets = owner * local_keys
    own_rows = lax.dynamic_slice_in_dim(sampled_rows, me * local_rows, local_rows, 0)
    own_rows = jnp.pad(own_rows, (0, extra - local_rows))[None, :]
    mask, turned = pl.pallas_call(
        prepare_kernel,
        out_shape=(
            jax.ShapeDtypeStruct((amount, extra), jnp.bfloat16),
            jax.ShapeDtypeStruct((groups, depth + extra, width), jnp.bfloat16),
        ),
        in_specs=[SCALARS, WHOLE, WHOLE],
        out_specs=(WHOLE, WHOLE),
        compiler_params=grant(8 if amount <= SPAN else 32),
        name="prepare",
    )(offsets, own_rows, query_vectors)
    stages = []
    for i, chosen in enumerate(early):
        some = len(chosen) * local_keys
        stages += pl.pallas_call(
            functools.partial(stage_kernel, i * some),
            out_shape=(
                jax.ShapeDtypeStruct((some, groups * width), jnp.float32),
                jax.ShapeDtypeStruct((1, groups * width), jnp.float32),
                jax.ShapeDtypeStruct((1, groups * width), jnp.float32),
            ),
            in_specs=[WHOLE] * (2 + len(chosen)),
            out_specs=(WHOLE,) * 3,
            scratch_shapes=[
                pltpu.VMEM((groups, some, depth), jnp.bfloat16),
                pltpu.VMEM((groups * local_keys, depth), jnp.float32),
                pltpu.VMEM((some, LANES), jnp.float32),
            ],
            compiler_params=grant(12),
        )(mask, turned, *blocks[2 * i : 2 * i + 2])
    blocks = blocks[2 * len(early) :]
    left = sum(counts) * local_keys
    partial = pl.pallas_call(
        functools.partial(column_kernel, counts, others, local_rows, len(early)),
        out_shape=jax.ShapeDtypeStruct((others * members, 1, local_keys), jnp.float32),
        in_specs=[SCALARS] + [WHOLE] * (2 + len(stages) + len(blocks)),
        out_specs=WHOLE,
        scratch_shapes=[
            pltpu.VMEM((groups, left, depth), jnp.bfloat16),
            pltpu.VMEM((groups * local_keys, depth), jnp.float32),
            pltpu.VMEM((amount, 128), jnp.float32),
        ]
        + [pltpu.VMEM((left, LANES), jnp.float32)] * (3 if left <= SPAN else 1),
        compiler_params=grant(24 if left <= SPAN else 60),
        name="columns",
    )(offsets, mask, turned, *stages, *blocks)
    received = lax.all_to_all(partial, ("kv", "seq"), 0, 0, tiled=True)
    return jnp.sum(received, axis=(0, 1))


def solution(mesh):
    placed = (P(), P("seq", "kv", None), P("seq", "kv", None))
    return jax.shard_map(on_device, mesh=mesh, in_specs=placed, out_specs=P("seq"), check_vma=False)
```

```python
import functools
import math

import jax
import jax.numpy as jnp
from jax import lax
from jax.experimental import pallas as pl
from jax.experimental.pallas import tpu as pltpu
from jax.sharding import PartitionSpec as P


NEG = -1e30
LOW = -1e20
SPAN = 2048
LANES = 256
CHUNK = 256
CONTRACT_LAST = (((1,), (1,)), ((), ()))
CONTRACT_INNER = (((1,), (0,)), ((), ()))
WHOLE = pl.BlockSpec(memory_space=pltpu.VMEM)


def grant(mebibytes):
    return pltpu.CompilerParams(vmem_limit_bytes=mebibytes << 20)


def round_up(value, step):
    return -(-value // step) * step


def owner_of(index, members, away):
    if away is None:
        return index
    return ((lax.axis_index("seq") + members + away[index // 2]) % members) ^ (index % 2)


def prepare_kernel(members, away, row_ref, query_ref, mask_ref, turned_ref):
    rows, heads, depth = query_ref.shape
    groups, _, width = turned_ref.shape
    size = heads // groups
    extra = mask_ref.shape[1]
    block = mask_ref.shape[0] // members
    column = lax.broadcasted_iota(jnp.int32, (block, extra), 1)
    place = lax.broadcasted_iota(jnp.int32, (block, extra), 0)
    first = lax.axis_index("seq") * rows
    back = lax.rem(row_ref.shape[1] - first, row_ref.shape[1])
    position = pltpu.roll(row_ref[...], back, 1)[:, :extra]

    def mask(index):
        hidden = (place + owner_of(index, members, away) * block > position) & (column < rows)
        value = jnp.where(hidden, NEG, 0.0)
        here = index * block
        here = here if away else pl.multiple_of(here, block)
        mask_ref[pl.ds(here, block), :] = value.astype(mask_ref.dtype)

    if away is None:
        pl.loop(0, members)(mask)
    else:
        for index in range(members):
            mask(index)
    wide = query_ref[...].astype(jnp.float32)
    eye = (
        lax.broadcasted_iota(jnp.int32, (depth, depth), 0)
        == lax.broadcasted_iota(jnp.int32, (depth, depth), 1)
    )
    eye = jnp.where(eye, 1.0, 0.0).astype(jnp.bfloat16)
    owner = lax.broadcasted_iota(jnp.int32, (extra, width), 1) // size
    hot = owner == lax.broadcasted_iota(jnp.int32, (extra, width), 0)
    hot = jnp.where(hot, 1.0, 0.0).astype(jnp.bfloat16)
    for g in range(groups):
        part = wide[:, g * size : (g + 1) * size, :].reshape(width, depth).astype(jnp.bfloat16)
        turned = lax.dot_general(eye, part, CONTRACT_LAST, preferred_element_type=jnp.float32)
        turned_ref[g, :depth, :] = turned.astype(turned_ref.dtype)
        turned_ref[g, depth:, :] = hot


def split_keys(key_refs, counts, keys, plain):
    groups = keys.shape[0]
    block = plain.shape[0] // groups

    def split(ref, index, first):
        plain[...] = ref[pl.ds(index * groups * block, groups * block), :].astype(jnp.float32)
        for g in range(groups):
            part = plain[pl.ds(g, block, stride=groups), :]
            keys[g, pl.ds(first, block), :] = part.astype(keys.dtype)

    done = 0
    for ref, count in zip(key_refs, counts, strict=True):
        if count == 1:
            split(ref, 0, done * block)
        else:

            @pl.loop(0, count)
            def _(i, ref=ref, done=done):
                split(ref, i, pl.multiple_of((done + i) * block, block))

        done += count


def tile_of(step, width):
    across = width // LANES
    first = (step % across) * LANES
    return step // across, pl.ds(pl.multiple_of(first, LANES), LANES)


def raw_scores(keys, mask_ref, turned_ref, step, here, base, held, top):
    g, lanes = tile_of(step, turned_ref.shape[2])
    shown = pl.ds(here.start + base, here.size)
    left = jnp.concatenate([keys[g, here, :], mask_ref[shown, :]], axis=1)
    value = lax.dot_general(
        left, turned_ref[g, :, lanes], CONTRACT_INNER, preferred_element_type=jnp.float32
    )
    held[here, :] = value
    return jnp.maximum(top, jnp.max(value.reshape(here.size // 8, 8, LANES), axis=0))


def stage_kernel(base, mask_ref, turned_ref, *refs):
    *key_refs, term_ref, top_ref, sum_ref, keys, plain, even, odd = refs
    amount, depth = keys.shape[1:]
    width = turned_ref.shape[2]
    chunk = math.gcd(amount, CHUNK)
    factor = math.log2(math.e) / math.sqrt(depth)
    split_keys(key_refs, [1] * len(key_refs), keys, plain)
    tiles = keys.shape[0] * (width // LANES)
    tops = {}
    for step in range(tiles + 1):
        top = jnp.full((8, LANES), LOW, jnp.float32)
        summed = jnp.zeros((8, LANES), jnp.float32)
        columns = pl.ds((step - 1) * LANES, LANES)
        for b in range(amount // chunk):
            here = pl.ds(b * chunk, chunk)
            if step:
                held = (even, odd)[(step - 1) % 2]
                value = jnp.exp2((held[here, :] - tops[step - 1]) * factor)
                term_ref[here, columns] = value
                summed = summed + jnp.sum(value.reshape(chunk // 8, 8, LANES), axis=0)
            if step < tiles:
                held = (even, odd)[step % 2]
                top = raw_scores(keys, mask_ref, turned_ref, step, here, base, held, top)
        if step:
            top_ref[:, columns] = tops[step - 1]
            sum_ref[:, columns] = jnp.sum(summed, axis=0, keepdims=True)
        tops[step] = jnp.max(top, axis=0, keepdims=True)


def column_kernel(members, away, counts, copies, rows, early, mask_ref, turned_ref, *refs):
    stages = [refs[3 * i : 3 * i + 3] for i in range(early)]
    refs = refs[3 * early :]
    key_refs, (out_ref, keys, plain, total, *scores) = refs[: len(counts)], refs[len(counts) :]
    groups, amount, depth = keys.shape
    width = turned_ref.shape[2]
    block = plain.shape[0] // groups
    chunk = math.gcd(amount, CHUNK)
    factor = math.log2(math.e) / math.sqrt(depth)
    every = total.shape[0]
    base = every - amount
    split_keys(key_refs, counts, keys, plain)
    tiles = groups * (width // LANES)

    def score(step, here, held, top):
        return raw_scores(keys, mask_ref, turned_ref, step, here, base, held, top)

    def term(here, held, top, summed):
        value = jnp.exp2((held[here, :] - top) * factor)
        held[here, :] = value
        return summed + jnp.sum(value.reshape(here.size // 8, 8, LANES), axis=0)

    def spread(value, weight, there, first):
        value = value * weight
        part = value[:, :128]
        for i in range(1, LANES // 128):
            part = part + value[:, i * 128 : (i + 1) * 128]
        total[there, :] = part if first else total[there, :] + part

    lowest = jnp.full((8, LANES), LOW, jnp.float32)
    nothing = jnp.zeros((8, LANES), jnp.float32)
    if amount <= SPAN:
        top, weights = {}, {}
        parts = amount // chunk
        for step in range(tiles + 2):
            high, summed = lowest, nothing
            old = step - 2
            for b in range(parts):
                here = pl.ds(b * chunk, chunk)
                if 0 <= old:
                    first = 0
                    columns = pl.ds(old * LANES, LANES)
                    for (terms, _, _), weight in zip(stages, weights[old][1:], strict=True):
                        size = terms.shape[0] // parts
                        value = terms[pl.ds(b * size, size), columns]
                        spread(value, weight, pl.ds(first + b * size, size), old == 0)
                        first += terms.shape[0]
                    value = scores[old % 3][here, :]
                    spread(value, weights[old][0], pl.ds(base + b * chunk, chunk), old == 0)
                if 0 <= step - 1 < tiles:
                    summed = term(here, scores[(step - 1) % 3], top[step - 1], summed)
                if step < tiles:
                    high = score(step, here, scores[step % 3], high)
            if 0 <= step - 1 < tiles:
                columns = pl.ds((step - 1) * LANES, LANES)
                whole = jnp.sum(summed, axis=0, keepdims=True)
                scale = [jnp.exp2((s[1][:, columns] - top[step - 1]) * factor) for s in stages]
                for s, by in zip(stages, scale, strict=True):
                    whole = whole + s[2][:, columns] * by
                share = 1.0 / whole
                weights[step - 1] = [share] + [share * by for by in scale]
            if step < tiles:
                columns = pl.ds(step * LANES, LANES)
                peak = jnp.max(high, axis=0, keepdims=True)
                for s in stages:
                    peak = jnp.maximum(peak, s[1][:, columns])
                top[step] = peak
    else:
        total[...] = jnp.zeros_like(total)

        def over(body, carry):
            def at(i, c):
                return body(pl.ds(pl.multiple_of(i * chunk, chunk), chunk), c)

            return lax.fori_loop(0, amount // chunk, at, carry)

        @pl.loop(0, tiles)
        def _(step):
            held = scores[0]
            high = over(lambda here, c: score(step, here, held, c), lowest)
            peak = jnp.max(high, axis=0, keepdims=True)
            summed = over(lambda here, c: term(here, held, peak, c), nothing)
            share = 1.0 / jnp.sum(summed, axis=0, keepdims=True)

            def last(here, c):
                spread(held[here, :], share, here, False)
                return c

            over(last, 0)

    ones = jnp.ones((16, 128), jnp.bfloat16)

    def finish(index):
        here = pl.ds(pl.multiple_of(index * block, block), block)
        high = total[here, :].astype(jnp.bfloat16)
        low = (total[here, :] - high.astype(jnp.float32)).astype(jnp.bfloat16)
        line = sum(
            lax.dot_general(ones, part, CONTRACT_LAST, preferred_element_type=jnp.float32)
            for part in (high, low)
        )[:1]
        row = owner_of(index, members, away)
        line = line * (1.0 / (width // rows))
        for i in range(copies):
            out_ref[i * (every // block) + row, :, :] = line

    if amount <= SPAN:
        for index in range(every // block):
            finish(index)
    else:
        pl.loop(0, every // block)(finish)


def gather_keys(key_vectors):
    size = lax.axis_size("seq")
    swap = [(i, i ^ 1) for i in range(size)]
    ahead = [(i, (i + 2) % size) for i in range(size)]
    blocks = {"own": key_vectors}
    blocks["left"] = lax.ppermute(key_vectors, "seq", ahead)
    blocks["right"] = lax.ppermute(key_vectors, "seq", [(j, i) for i, j in ahead])
    blocks["far"] = lax.ppermute(blocks["left"], "seq", ahead)
    found = []
    for block in blocks.values():
        found += [block, lax.ppermute(block, "seq", swap)]
    return found, (0, -2, 2, -4)


def on_device(sampled_rows, query_vectors, key_vectors):
    local_rows, heads, depth = query_vectors.shape
    local_keys, groups, _ = key_vectors.shape
    width = local_rows * heads // groups
    members = lax.axis_size("seq")
    others = lax.axis_size("kv")
    amount = members * local_keys
    extra = round_up(local_rows, 128)
    if members == 8:
        blocks, away = gather_keys(key_vectors)
        early, counts = 2, [1] * 4
    else:
        blocks, away = [lax.all_gather(key_vectors, "seq", axis=0, tiled=True)], None
        early, counts = 0, [members]
    blocks = [b.reshape(-1, depth) for b in blocks]
    mask, turned = pl.pallas_call(
        functools.partial(prepare_kernel, members, away),
        out_shape=(
            jax.ShapeDtypeStruct((amount, extra), jnp.bfloat16),
            jax.ShapeDtypeStruct((groups, depth + extra, width), jnp.bfloat16),
        ),
        in_specs=[WHOLE, WHOLE],
        out_specs=(WHOLE, WHOLE),
        compiler_params=grant(8 if amount <= SPAN else 32),
        name="prepare",
    )(sampled_rows[None, :], query_vectors)
    stages = []
    some = 2 * local_keys
    for i in range(early):
        stages += pl.pallas_call(
            functools.partial(stage_kernel, i * some),
            out_shape=(
                jax.ShapeDtypeStruct((some, groups * width), jnp.float32),
                jax.ShapeDtypeStruct((1, groups * width), jnp.float32),
                jax.ShapeDtypeStruct((1, groups * width), jnp.float32),
            ),
            in_specs=[WHOLE] * 4,
            out_specs=(WHOLE,) * 3,
            scratch_shapes=[
                pltpu.VMEM((groups, some, depth), jnp.bfloat16),
                pltpu.VMEM((groups * local_keys, depth), jnp.float32),
            ]
            + [pltpu.VMEM((some, LANES), jnp.float32)] * 2,
            compiler_params=grant(12),
        )(mask, turned, *blocks[2 * i : 2 * i + 2])
    blocks = blocks[2 * early :]
    left = sum(counts) * local_keys
    partial = pl.pallas_call(
        functools.partial(column_kernel, members, away, counts, others, local_rows, early),
        out_shape=jax.ShapeDtypeStruct((others * members, 1, local_keys), jnp.float32),
        in_specs=[WHOLE] * (2 + len(stages) + len(blocks)),
        out_specs=WHOLE,
        scratch_shapes=[
            pltpu.VMEM((groups, left, depth), jnp.bfloat16),
            pltpu.VMEM((groups * local_keys, depth), jnp.float32),
            pltpu.VMEM((amount, 128), jnp.float32),
        ]
        + [pltpu.VMEM((left, LANES), jnp.float32)] * (3 if left <= SPAN else 1),
        compiler_params=grant(24 if left <= SPAN else 60),
        name="columns",
    )(mask, turned, *stages, *blocks)
    received = lax.all_to_all(partial, ("kv", "seq"), 0, 0, tiled=True)
    return jnp.sum(received, axis=(0, 1))


def solution(mesh):
    placed = (P(), P("seq", "kv", None), P("seq", "kv", None))
    return jax.shard_map(on_device, mesh=mesh, in_specs=placed, out_specs=P("seq"), check_vma=False)
```

```python
import functools
import math

import jax
import jax.numpy as jnp
from jax import lax
from jax.experimental import pallas as pl
from jax.experimental.pallas import tpu as pltpu
from jax.sharding import PartitionSpec as P


NEG = -1e30
LOW = -1e20
SPAN = 2048
LANES = 256
CHUNK = 256
CONTRACT_LAST = (((1,), (1,)), ((), ()))
CONTRACT_INNER = (((1,), (0,)), ((), ()))
WHOLE = pl.BlockSpec(memory_space=pltpu.VMEM)
ANYWHERE = pl.BlockSpec(memory_space=pltpu.HBM)


def grant(mebibytes):
    return pltpu.CompilerParams(vmem_limit_bytes=mebibytes << 20)


def round_up(value, step):
    return -(-value // step) * step


def owner_of(index, members, away):
    if away is None:
        return index
    return ((lax.axis_index("seq") + members + away[index // 2]) % members) ^ (index % 2)


def prepare_kernel(members, away, row_ref, query_hbm, key_hbm, mask_ref, turned_ref, key_ref, query_ref, sem):
    rows, heads, depth = query_ref.shape
    groups, _, width = turned_ref.shape
    fetch_query = pltpu.make_async_copy(query_hbm, query_ref, sem.at[0])
    fetch_key = pltpu.make_async_copy(key_hbm, key_ref, sem.at[1])
    fetch_query.start()
    fetch_key.start()
    size = heads // groups
    extra = mask_ref.shape[1]
    block = mask_ref.shape[0] // members
    column = lax.broadcasted_iota(jnp.int32, (block, extra), 1)
    place = lax.broadcasted_iota(jnp.int32, (block, extra), 0)
    first = lax.axis_index("seq") * rows
    total = row_ref.shape[0]
    back = lax.rem(total - first, total)
    position = pltpu.roll(row_ref[...].reshape(1, total), back, 1)[:, :extra]

    def mask(index):
        hidden = (place + owner_of(index, members, away) * block > position) & (column < rows)
        value = jnp.where(hidden, NEG, 0.0)
        here = index * block
        here = here if away else pl.multiple_of(here, block)
        mask_ref[pl.ds(here, block), :] = value.astype(mask_ref.dtype)

    if away is None:
        pl.loop(0, members)(mask)
    else:
        for index in range(members):
            mask(index)
    fetch_query.wait()
    wide = query_ref[...].astype(jnp.float32)
    eye = (
        lax.broadcasted_iota(jnp.int32, (depth, depth), 0)
        == lax.broadcasted_iota(jnp.int32, (depth, depth), 1)
    )
    eye = jnp.where(eye, 1.0, 0.0).astype(jnp.bfloat16)
    owner = lax.broadcasted_iota(jnp.int32, (extra, width), 1) // size
    hot = owner == lax.broadcasted_iota(jnp.int32, (extra, width), 0)
    hot = jnp.where(hot, 1.0, 0.0).astype(jnp.bfloat16)
    for g in range(groups):
        part = wide[:, g * size : (g + 1) * size, :].reshape(width, depth).astype(jnp.bfloat16)
        turned = lax.dot_general(eye, part, CONTRACT_LAST, preferred_element_type=jnp.float32)
        turned_ref[g, :depth, :] = turned.astype(turned_ref.dtype)
        turned_ref[g, depth:, :] = hot
    fetch_key.wait()


def split_keys(key_refs, counts, keys, plain):
    groups = keys.shape[0]
    block = plain.shape[0] // groups

    def split(ref, index, first):
        plain[...] = ref[pl.ds(index * groups * block, groups * block), :].astype(jnp.float32)
        for g in range(groups):
            part = plain[pl.ds(g, block, stride=groups), :]
            keys[g, pl.ds(first, block), :] = part.astype(keys.dtype)

    done = 0
    for ref, count in zip(key_refs, counts, strict=True):
        if count == 1:
            split(ref, 0, done * block)
        else:

            @pl.loop(0, count)
            def _(i, ref=ref, done=done):
                split(ref, i, pl.multiple_of((done + i) * block, block))

        done += count


def tile_of(step, width):
    across = width // LANES
    first = (step % across) * LANES
    return step // across, pl.ds(pl.multiple_of(first, LANES), LANES)


def raw_scores(keys, mask_ref, turned_ref, step, here, base, held, top):
    g, lanes = tile_of(step, turned_ref.shape[2])
    shown = pl.ds(here.start + base, here.size)
    left = jnp.concatenate([keys[g, here, :], mask_ref[shown, :]], axis=1)
    value = lax.dot_general(
        left, turned_ref[g, :, lanes], CONTRACT_INNER, preferred_element_type=jnp.float32
    )
    held[here, :] = value
    return jnp.maximum(top, jnp.max(value.reshape(here.size // 8, 8, LANES), axis=0))


def stage_kernel(base, mask_ref, turned_ref, *refs):
    *key_refs, term_ref, top_ref, sum_ref, keys, plain, even, odd = refs
    amount, depth = keys.shape[1:]
    width = turned_ref.shape[2]
    chunk = math.gcd(amount, CHUNK)
    factor = math.log2(math.e) / math.sqrt(depth)
    split_keys(key_refs, [1] * len(key_refs), keys, plain)
    tiles = keys.shape[0] * (width // LANES)
    tops = {}
    for step in range(tiles + 1):
        top = jnp.full((8, LANES), LOW, jnp.float32)
        summed = jnp.zeros((8, LANES), jnp.float32)
        columns = pl.ds((step - 1) * LANES, LANES)
        for b in range(amount // chunk):
            here = pl.ds(b * chunk, chunk)
            if step:
                held = (even, odd)[(step - 1) % 2]
                value = jnp.exp2((held[here, :] - tops[step - 1]) * factor)
                term_ref[here, columns] = value
                summed = summed + jnp.sum(value.reshape(chunk // 8, 8, LANES), axis=0)
            if step < tiles:
                held = (even, odd)[step % 2]
                top = raw_scores(keys, mask_ref, turned_ref, step, here, base, held, top)
        if step:
            top_ref[:, columns] = tops[step - 1]
            sum_ref[:, columns] = jnp.sum(summed, axis=0, keepdims=True)
        tops[step] = jnp.max(top, axis=0, keepdims=True)


def column_kernel(members, away, counts, copies, rows, early, mask_ref, turned_ref, *refs):
    stages = [refs[3 * i : 3 * i + 3] for i in range(early)]
    refs = refs[3 * early :]
    key_refs, (out_ref, keys, plain, total, *scores) = refs[: len(counts)], refs[len(counts) :]
    groups, amount, depth = keys.shape
    width = turned_ref.shape[2]
    block = plain.shape[0] // groups
    chunk = math.gcd(amount, CHUNK)
    factor = math.log2(math.e) / math.sqrt(depth)
    every = total.shape[0]
    base = every - amount
    split_keys(key_refs, counts, keys, plain)
    tiles = groups * (width // LANES)

    def score(step, here, held, top):
        return raw_scores(keys, mask_ref, turned_ref, step, here, base, held, top)

    def term(here, held, top, summed):
        value = jnp.exp2((held[here, :] - top) * factor)
        held[here, :] = value
        return summed + jnp.sum(value.reshape(here.size // 8, 8, LANES), axis=0)

    def spread(value, weight, there, first):
        value = value * weight
        part = value[:, :128]
        for i in range(1, LANES // 128):
            part = part + value[:, i * 128 : (i + 1) * 128]
        total[there, :] = part if first else total[there, :] + part

    lowest = jnp.full((8, LANES), LOW, jnp.float32)
    nothing = jnp.zeros((8, LANES), jnp.float32)
    if amount <= SPAN:
        top, weights = {}, {}
        parts = amount // chunk
        for step in range(tiles + 2):
            high, summed = lowest, nothing
            old = step - 2
            for b in range(parts):
                here = pl.ds(b * chunk, chunk)
                if 0 <= old:
                    first = 0
                    columns = pl.ds(old * LANES, LANES)
                    for (terms, _, _), weight in zip(stages, weights[old][1:], strict=True):
                        size = terms.shape[0] // parts
                        value = terms[pl.ds(b * size, size), columns]
                        spread(value, weight, pl.ds(first + b * size, size), old == 0)
                        first += terms.shape[0]
                    value = scores[old % 3][here, :]
                    spread(value, weights[old][0], pl.ds(base + b * chunk, chunk), old == 0)
                if 0 <= step - 1 < tiles:
                    summed = term(here, scores[(step - 1) % 3], top[step - 1], summed)
                if step < tiles:
                    high = score(step, here, scores[step % 3], high)
            if 0 <= step - 1 < tiles:
                columns = pl.ds((step - 1) * LANES, LANES)
                whole = jnp.sum(summed, axis=0, keepdims=True)
                scale = [jnp.exp2((s[1][:, columns] - top[step - 1]) * factor) for s in stages]
                for s, by in zip(stages, scale, strict=True):
                    whole = whole + s[2][:, columns] * by
                share = 1.0 / whole
                weights[step - 1] = [share] + [share * by for by in scale]
            if step < tiles:
                columns = pl.ds(step * LANES, LANES)
                peak = jnp.max(high, axis=0, keepdims=True)
                for s in stages:
                    peak = jnp.maximum(peak, s[1][:, columns])
                top[step] = peak
    else:
        total[...] = jnp.zeros_like(total)

        def over(body, carry):
            def at(i, c):
                return body(pl.ds(pl.multiple_of(i * chunk, chunk), chunk), c)

            return lax.fori_loop(0, amount // chunk, at, carry)

        @pl.loop(0, tiles)
        def _(step):
            held = scores[0]
            high = over(lambda here, c: score(step, here, held, c), lowest)
            peak = jnp.max(high, axis=0, keepdims=True)
            summed = over(lambda here, c: term(here, held, peak, c), nothing)
            share = 1.0 / jnp.sum(summed, axis=0, keepdims=True)

            def last(here, c):
                spread(held[here, :], share, here, False)
                return c

            over(last, 0)

    ones = jnp.ones((16, 128), jnp.bfloat16)

    def finish(index):
        here = pl.ds(pl.multiple_of(index * block, block), block)
        high = total[here, :].astype(jnp.bfloat16)
        low = (total[here, :] - high.astype(jnp.float32)).astype(jnp.bfloat16)
        line = sum(
            lax.dot_general(ones, part, CONTRACT_LAST, preferred_element_type=jnp.float32)
            for part in (high, low)
        )[:1]
        row = owner_of(index, members, away)
        line = line * (1.0 / (width // rows))
        for i in range(copies):
            out_ref[i * (every // block) + row, :, :] = line

    if amount <= SPAN:
        for index in range(every // block):
            finish(index)
    else:
        pl.loop(0, every // block)(finish)


def gather_keys(key_vectors):
    size = lax.axis_size("seq")
    swap = [(i, i ^ 1) for i in range(size)]
    ahead = [(i, (i + 2) % size) for i in range(size)]
    blocks = {"own": key_vectors}
    blocks["left"] = lax.ppermute(key_vectors, "seq", ahead)
    blocks["right"] = lax.ppermute(key_vectors, "seq", [(j, i) for i, j in ahead])
    blocks["far"] = lax.ppermute(blocks["left"], "seq", ahead)
    found = []
    for block in blocks.values():
        found += [block, lax.ppermute(block, "seq", swap)]
    return found, (0, -2, 2, -4)


def on_device(sampled_rows, query_vectors, key_vectors):
    local_rows, heads, depth = query_vectors.shape
    local_keys, groups, _ = key_vectors.shape
    width = local_rows * heads // groups
    members = lax.axis_size("seq")
    others = lax.axis_size("kv")
    amount = members * local_keys
    extra = round_up(local_rows, 128)
    if members == 8:
        blocks, away = gather_keys(key_vectors)
        early, counts = 3, [1] * 2
    else:
        blocks, away = [lax.all_gather(key_vectors, "seq", axis=0, tiled=True)], None
        early, counts = 0, [members]
    blocks = [b.reshape(-1, depth) for b in blocks]
    mask, turned, own = pl.pallas_call(
        functools.partial(prepare_kernel, members, away),
        out_shape=(
            jax.ShapeDtypeStruct((amount, extra), jnp.bfloat16),
            jax.ShapeDtypeStruct((groups, depth + extra, width), jnp.bfloat16),
            jax.ShapeDtypeStruct((local_keys * groups, depth), jnp.bfloat16),
        ),
        in_specs=[WHOLE, ANYWHERE, ANYWHERE],
        out_specs=(WHOLE, WHOLE, WHOLE),
        scratch_shapes=[
            pltpu.VMEM(query_vectors.shape, jnp.bfloat16),
            pltpu.SemaphoreType.DMA((2,)),
        ],
        compiler_params=grant(8 if amount <= SPAN else 32),
        name="prepare",
    )(
        sampled_rows,
        pltpu.with_memory_space_constraint(query_vectors, pltpu.HBM),
        pltpu.with_memory_space_constraint(key_vectors.reshape(-1, depth), pltpu.HBM),
    )
    if early:
        blocks[0] = own
    stages = []
    some = 2 * local_keys
    for i in range(early):
        stages += pl.pallas_call(
            functools.partial(stage_kernel, i * some),
            out_shape=(
                jax.ShapeDtypeStruct((some, groups * width), jnp.float32),
                jax.ShapeDtypeStruct((1, groups * width), jnp.float32),
                jax.ShapeDtypeStruct((1, groups * width), jnp.float32),
            ),
            in_specs=[WHOLE] * 4,
            out_specs=(WHOLE,) * 3,
            scratch_shapes=[
                pltpu.VMEM((groups, some, depth), jnp.bfloat16),
                pltpu.VMEM((groups * local_keys, depth), jnp.float32),
            ]
            + [pltpu.VMEM((some, LANES), jnp.float32)] * 2,
            compiler_params=grant(12),
        )(mask, turned, *blocks[2 * i : 2 * i + 2])
    blocks = blocks[2 * early :]
    left = sum(counts) * local_keys
    partial = pl.pallas_call(
        functools.partial(column_kernel, members, away, counts, others, local_rows, early),
        out_shape=jax.ShapeDtypeStruct((others * members, 1, local_keys), jnp.float32),
        in_specs=[WHOLE] * (2 + len(stages) + len(blocks)),
        out_specs=WHOLE,
        scratch_shapes=[
            pltpu.VMEM((groups, left, depth), jnp.bfloat16),
            pltpu.VMEM((groups * local_keys, depth), jnp.float32),
            pltpu.VMEM((amount, 128), jnp.float32),
        ]
        + [pltpu.VMEM((left, LANES), jnp.float32)] * (3 if left <= SPAN else 1),
        compiler_params=grant(24 if left <= SPAN else 60),
        name="columns",
    )(mask, turned, *stages, *blocks)
    received = lax.all_to_all(partial, ("kv", "seq"), 0, 0, tiled=True)
    return jnp.sum(received, axis=(0, 1))


def solution(mesh):
    placed = (P(), P("seq", "kv", None), P("seq", "kv", None))
    return jax.shard_map(on_device, mesh=mesh, in_specs=placed, out_specs=P("seq"), check_vma=False)
```

```python
import functools
import math

import jax
import jax.numpy as jnp
from jax import lax
from jax.experimental import pallas as pl
from jax.experimental.pallas import tpu as pltpu
from jax.sharding import PartitionSpec as P


NEG = -1e30
LOW = -1e20
SPAN = 2048
LANES = 256
CHUNK = 256
CONTRACT_LAST = (((1,), (1,)), ((), ()))
CONTRACT_INNER = (((1,), (0,)), ((), ()))
WHOLE = pl.BlockSpec(memory_space=pltpu.VMEM)
ANYWHERE = pl.BlockSpec(memory_space=pltpu.HBM)


def grant(mebibytes):
    return pltpu.CompilerParams(vmem_limit_bytes=mebibytes << 20)


def round_up(value, step):
    return -(-value // step) * step


def owner_of(index, owners):
    if owners is None:
        return index
    me = lax.axis_index("seq")
    chip = sum(jnp.where(me // 2 == i, owner, 0) for i, owner in enumerate(owners[index // 2]))
    return 2 * chip + ((me % 2) ^ (index % 2))


def prepare_kernel(members, owners, row_ref, query_hbm, key_hbm, mask_ref, turned_ref, key_ref, query_ref, sem):
    rows, heads, depth = query_ref.shape
    groups, _, width = turned_ref.shape
    fetch_query = pltpu.make_async_copy(query_hbm, query_ref, sem.at[0])
    fetch_key = pltpu.make_async_copy(key_hbm, key_ref, sem.at[1])
    fetch_query.start()
    fetch_key.start()
    size = heads // groups
    extra = mask_ref.shape[1]
    block = mask_ref.shape[0] // members
    column = lax.broadcasted_iota(jnp.int32, (block, extra), 1)
    place = lax.broadcasted_iota(jnp.int32, (block, extra), 0)
    first = lax.axis_index("seq") * rows
    total = row_ref.shape[0]
    back = lax.rem(total - first, total)
    position = pltpu.roll(row_ref[...].reshape(1, total), back, 1)[:, :extra]

    def mask(index):
        hidden = (place + owner_of(index, owners) * block > position) & (column < rows)
        value = jnp.where(hidden, NEG, 0.0)
        here = index * block
        here = here if owners else pl.multiple_of(here, block)
        mask_ref[pl.ds(here, block), :] = value.astype(mask_ref.dtype)

    if owners is None:
        pl.loop(0, members)(mask)
    else:
        for index in range(members):
            mask(index)
    fetch_query.wait()
    wide = query_ref[...].astype(jnp.float32)
    eye = (
        lax.broadcasted_iota(jnp.int32, (depth, depth), 0)
        == lax.broadcasted_iota(jnp.int32, (depth, depth), 1)
    )
    eye = jnp.where(eye, 1.0, 0.0).astype(jnp.bfloat16)
    owner = lax.broadcasted_iota(jnp.int32, (extra, width), 1) // size
    hot = owner == lax.broadcasted_iota(jnp.int32, (extra, width), 0)
    hot = jnp.where(hot, 1.0, 0.0).astype(jnp.bfloat16)
    for g in range(groups):
        part = wide[:, g * size : (g + 1) * size, :].reshape(width, depth).astype(jnp.bfloat16)
        turned = lax.dot_general(eye, part, CONTRACT_LAST, preferred_element_type=jnp.float32)
        turned_ref[g, :depth, :] = turned.astype(turned_ref.dtype)
        turned_ref[g, depth:, :] = hot
    fetch_key.wait()


def split_keys(key_refs, counts, keys, plain):
    groups = keys.shape[0]
    block = plain.shape[0] // groups

    def split(ref, index, first):
        plain[...] = ref[pl.ds(index * groups * block, groups * block), :].astype(jnp.float32)
        for g in range(groups):
            part = plain[pl.ds(g, block, stride=groups), :]
            keys[g, pl.ds(first, block), :] = part.astype(keys.dtype)

    done = 0
    for ref, count in zip(key_refs, counts, strict=True):
        if count == 1:
            split(ref, 0, done * block)
        else:

            @pl.loop(0, count)
            def _(i, ref=ref, done=done):
                split(ref, i, pl.multiple_of((done + i) * block, block))

        done += count


def tile_of(step, width):
    across = width // LANES
    first = (step % across) * LANES
    return step // across, pl.ds(pl.multiple_of(first, LANES), LANES)


def raw_scores(keys, mask_ref, turned_ref, step, here, base, held, top):
    g, lanes = tile_of(step, turned_ref.shape[2])
    shown = pl.ds(here.start + base, here.size)
    left = jnp.concatenate([keys[g, here, :], mask_ref[shown, :]], axis=1)
    value = lax.dot_general(
        left, turned_ref[g, :, lanes], CONTRACT_INNER, preferred_element_type=jnp.float32
    )
    held[here, :] = value
    return jnp.maximum(top, jnp.max(value.reshape(here.size // 8, 8, LANES), axis=0))


def stage_kernel(base, mask_ref, turned_ref, *refs):
    *key_refs, term_ref, top_ref, sum_ref, keys, plain, even, odd = refs
    amount, depth = keys.shape[1:]
    width = turned_ref.shape[2]
    chunk = math.gcd(amount, CHUNK)
    factor = math.log2(math.e) / math.sqrt(depth)
    split_keys(key_refs, [1] * len(key_refs), keys, plain)
    tiles = keys.shape[0] * (width // LANES)
    tops = {}
    for step in range(tiles + 1):
        top = jnp.full((8, LANES), LOW, jnp.float32)
        summed = jnp.zeros((8, LANES), jnp.float32)
        columns = pl.ds((step - 1) * LANES, LANES)
        for b in range(amount // chunk):
            here = pl.ds(b * chunk, chunk)
            if step:
                held = (even, odd)[(step - 1) % 2]
                value = jnp.exp2((held[here, :] - tops[step - 1]) * factor)
                term_ref[here, columns] = value
                summed = summed + jnp.sum(value.reshape(chunk // 8, 8, LANES), axis=0)
            if step < tiles:
                held = (even, odd)[step % 2]
                top = raw_scores(keys, mask_ref, turned_ref, step, here, base, held, top)
        if step:
            top_ref[:, columns] = tops[step - 1]
            sum_ref[:, columns] = jnp.sum(summed, axis=0, keepdims=True)
        tops[step] = jnp.max(top, axis=0, keepdims=True)


def column_kernel(owners, counts, copies, rows, early, mask_ref, turned_ref, *refs):
    stages = [refs[3 * i : 3 * i + 3] for i in range(early)]
    refs = refs[3 * early :]
    key_refs, (out_ref, keys, plain, total, *scores) = refs[: len(counts)], refs[len(counts) :]
    groups, amount, depth = keys.shape
    width = turned_ref.shape[2]
    block = plain.shape[0] // groups
    chunk = math.gcd(amount, CHUNK)
    factor = math.log2(math.e) / math.sqrt(depth)
    every = total.shape[0]
    base = every - amount
    split_keys(key_refs, counts, keys, plain)
    tiles = groups * (width // LANES)

    def score(step, here, held, top):
        return raw_scores(keys, mask_ref, turned_ref, step, here, base, held, top)

    def term(here, held, top, summed):
        value = jnp.exp2((held[here, :] - top) * factor)
        held[here, :] = value
        return summed + jnp.sum(value.reshape(here.size // 8, 8, LANES), axis=0)

    def spread(value, weight, there, first):
        value = value * weight
        part = value[:, :128]
        for i in range(1, LANES // 128):
            part = part + value[:, i * 128 : (i + 1) * 128]
        total[there, :] = part if first else total[there, :] + part

    lowest = jnp.full((8, LANES), LOW, jnp.float32)
    nothing = jnp.zeros((8, LANES), jnp.float32)
    if amount <= SPAN:
        top, weights = {}, {}
        parts = amount // chunk
        for step in range(tiles + 2):
            high, summed = lowest, nothing
            old = step - 2
            for b in range(parts):
                here = pl.ds(b * chunk, chunk)
                if 0 <= old:
                    first = 0
                    columns = pl.ds(old * LANES, LANES)
                    for (terms, _, _), weight in zip(stages, weights[old][1:], strict=True):
                        size = terms.shape[0] // parts
                        value = terms[pl.ds(b * size, size), columns]
                        spread(value, weight, pl.ds(first + b * size, size), old == 0)
                        first += terms.shape[0]
                    value = scores[old % 3][here, :]
                    spread(value, weights[old][0], pl.ds(base + b * chunk, chunk), old == 0)
                if 0 <= step - 1 < tiles:
                    summed = term(here, scores[(step - 1) % 3], top[step - 1], summed)
                if step < tiles:
                    high = score(step, here, scores[step % 3], high)
            if 0 <= step - 1 < tiles:
                columns = pl.ds((step - 1) * LANES, LANES)
                whole = jnp.sum(summed, axis=0, keepdims=True)
                scale = [jnp.exp2((s[1][:, columns] - top[step - 1]) * factor) for s in stages]
                for s, by in zip(stages, scale, strict=True):
                    whole = whole + s[2][:, columns] * by
                share = 1.0 / whole
                weights[step - 1] = [share] + [share * by for by in scale]
            if step < tiles:
                columns = pl.ds(step * LANES, LANES)
                peak = jnp.max(high, axis=0, keepdims=True)
                for s in stages:
                    peak = jnp.maximum(peak, s[1][:, columns])
                top[step] = peak
    else:
        total[...] = jnp.zeros_like(total)

        def over(body, carry):
            def at(i, c):
                return body(pl.ds(pl.multiple_of(i * chunk, chunk), chunk), c)

            return lax.fori_loop(0, amount // chunk, at, carry)

        @pl.loop(0, tiles)
        def _(step):
            held = scores[0]
            high = over(lambda here, c: score(step, here, held, c), lowest)
            peak = jnp.max(high, axis=0, keepdims=True)
            summed = over(lambda here, c: term(here, held, peak, c), nothing)
            share = 1.0 / jnp.sum(summed, axis=0, keepdims=True)

            def last(here, c):
                spread(held[here, :], share, here, False)
                return c

            over(last, 0)

    ones = jnp.ones((16, 128), jnp.bfloat16)

    def finish(index):
        here = pl.ds(pl.multiple_of(index * block, block), block)
        high = total[here, :].astype(jnp.bfloat16)
        low = (total[here, :] - high.astype(jnp.float32)).astype(jnp.bfloat16)
        line = sum(
            lax.dot_general(ones, part, CONTRACT_LAST, preferred_element_type=jnp.float32)
            for part in (high, low)
        )[:1]
        row = owner_of(index, owners)
        line = line * (1.0 / (width // rows))
        for i in range(copies):
            out_ref[i * (every // block) + row, :, :] = line

    if amount <= SPAN:
        for index in range(every // block):
            finish(index)
    else:
        pl.loop(0, every // block)(finish)


def ring_of(chips):
    return list(range(0, chips, 2)) + list(range(1, chips, 2))[::-1]


def gather_keys(key_vectors):
    size = lax.axis_size("seq")
    ring = ring_of(size // 2)
    place = {chip: i for i, chip in enumerate(ring)}

    def chip_at(chip, steps):
        return ring[(place[chip] + steps) % len(ring)]

    swap = [(i, i ^ 1) for i in range(size)]
    ahead = [(i, 2 * chip_at(i // 2, 1) + i % 2) for i in range(size)]
    blocks = {"own": key_vectors}
    blocks["left"] = lax.ppermute(key_vectors, "seq", ahead)
    blocks["right"] = lax.ppermute(key_vectors, "seq", sorted((j, i) for i, j in ahead))
    blocks["far"] = lax.ppermute(blocks["left"], "seq", ahead)
    found = []
    for block in blocks.values():
        found += [block, lax.ppermute(block, "seq", swap)]
    return found, [[chip_at(i, by) for i in range(size // 2)] for by in (0, -1, 1, -2)]


def on_device(sampled_rows, query_vectors, key_vectors):
    local_rows, heads, depth = query_vectors.shape
    local_keys, groups, _ = key_vectors.shape
    width = local_rows * heads // groups
    members = lax.axis_size("seq")
    others = lax.axis_size("kv")
    amount = members * local_keys
    extra = round_up(local_rows, 128)
    if members == 8:
        blocks, owners = gather_keys(key_vectors)
        early, counts = 3, [1] * 2
    else:
        blocks, owners = [lax.all_gather(key_vectors, "seq", axis=0, tiled=True)], None
        early, counts = 0, [members]
    blocks = [b.reshape(-1, depth) for b in blocks]
    mask, turned, own = pl.pallas_call(
        functools.partial(prepare_kernel, members, owners),
        out_shape=(
            jax.ShapeDtypeStruct((amount, extra), jnp.bfloat16),
            jax.ShapeDtypeStruct((groups, depth + extra, width), jnp.bfloat16),
            jax.ShapeDtypeStruct((local_keys * groups, depth), jnp.bfloat16),
        ),
        in_specs=[WHOLE, ANYWHERE, ANYWHERE],
        out_specs=(WHOLE, WHOLE, WHOLE),
        scratch_shapes=[
            pltpu.VMEM(query_vectors.shape, jnp.bfloat16),
            pltpu.SemaphoreType.DMA((2,)),
        ],
        compiler_params=grant(8 if amount <= SPAN else 32),
        name="prepare",
    )(
        sampled_rows,
        pltpu.with_memory_space_constraint(query_vectors, pltpu.HBM),
        pltpu.with_memory_space_constraint(key_vectors.reshape(-1, depth), pltpu.HBM),
    )
    if early:
        blocks[0] = own
    stages = []
    some = 2 * local_keys
    for i in range(early):
        stages += pl.pallas_call(
            functools.partial(stage_kernel, i * some),
            out_shape=(
                jax.ShapeDtypeStruct((some, groups * width), jnp.float32),
                jax.ShapeDtypeStruct((1, groups * width), jnp.float32),
                jax.ShapeDtypeStruct((1, groups * width), jnp.float32),
            ),
            in_specs=[WHOLE] * 4,
            out_specs=(WHOLE,) * 3,
            scratch_shapes=[
                pltpu.VMEM((groups, some, depth), jnp.bfloat16),
                pltpu.VMEM((groups * local_keys, depth), jnp.float32),
            ]
            + [pltpu.VMEM((some, LANES), jnp.float32)] * 2,
            compiler_params=grant(12),
        )(mask, turned, *blocks[2 * i : 2 * i + 2])
    blocks = blocks[2 * early :]
    left = sum(counts) * local_keys
    partial = pl.pallas_call(
        functools.partial(column_kernel, owners, counts, others, local_rows, early),
        out_shape=jax.ShapeDtypeStruct((others * members, 1, local_keys), jnp.float32),
        in_specs=[WHOLE] * (2 + len(stages) + len(blocks)),
        out_specs=WHOLE,
        scratch_shapes=[
            pltpu.VMEM((groups, left, depth), jnp.bfloat16),
            pltpu.VMEM((groups * local_keys, depth), jnp.float32),
            pltpu.VMEM((amount, 128), jnp.float32),
        ]
        + [pltpu.VMEM((left, LANES), jnp.float32)] * (3 if left <= SPAN else 1),
        compiler_params=grant(24 if left <= SPAN else 60),
        name="columns",
    )(mask, turned, *stages, *blocks)
    received = lax.all_to_all(partial, ("kv", "seq"), 0, 0, tiled=True)
    return jnp.sum(received, axis=(0, 1))


def solution(mesh):
    placed = (P(), P("seq", "kv", None), P("seq", "kv", None))
    return jax.shard_map(on_device, mesh=mesh, in_specs=placed, out_specs=P("seq"), check_vma=False)
```

```python
import functools
import math

import jax
import jax.numpy as jnp
from jax import lax
from jax.experimental import pallas as pl
from jax.experimental.pallas import tpu as pltpu
from jax.sharding import PartitionSpec as P


NEG = -1e30
LOW = -1e20
SPAN = 2048
LANES = 256
CHUNK = 128
CONTRACT_LAST = (((1,), (1,)), ((), ()))
CONTRACT_INNER = (((1,), (0,)), ((), ()))
WHOLE = pl.BlockSpec(memory_space=pltpu.VMEM)
ANYWHERE = pl.BlockSpec(memory_space=pltpu.HBM)


def grant(mebibytes):
    return pltpu.CompilerParams(vmem_limit_bytes=mebibytes << 20)


def round_up(value, step):
    return -(-value // step) * step


def owner_of(index, owners):
    if owners is None:
        return index
    me = lax.axis_index("seq")
    chip = sum(jnp.where(me // 2 == i, owner, 0) for i, owner in enumerate(owners[index // 2]))
    return 2 * chip + ((me % 2) ^ (index % 2))


def prepare_kernel(members, owners, row_ref, query_hbm, key_hbm, mask_ref, turned_ref, key_ref, query_ref, sem):
    rows, heads, depth = query_ref.shape
    groups, _, width = turned_ref.shape
    fetch_query = pltpu.make_async_copy(query_hbm, query_ref, sem.at[0])
    fetch_key = pltpu.make_async_copy(key_hbm, key_ref, sem.at[1])
    fetch_query.start()
    fetch_key.start()
    size = heads // groups
    extra = mask_ref.shape[1]
    block = mask_ref.shape[0] // members
    column = lax.broadcasted_iota(jnp.int32, (block, extra), 1)
    place = lax.broadcasted_iota(jnp.int32, (block, extra), 0)
    first = lax.axis_index("seq") * rows
    total = row_ref.shape[0]
    back = lax.rem(total - first, total)
    position = pltpu.roll(row_ref[...].reshape(1, total), back, 1)[:, :extra]

    def mask(index):
        hidden = (place + owner_of(index, owners) * block > position) & (column < rows)
        value = jnp.where(hidden, NEG, 0.0)
        here = index * block
        here = here if owners else pl.multiple_of(here, block)
        mask_ref[pl.ds(here, block), :] = value.astype(mask_ref.dtype)

    if owners is None:
        pl.loop(0, members)(mask)
    else:
        for index in range(members):
            mask(index)
    fetch_query.wait()
    wide = query_ref[...].astype(jnp.float32)
    eye = (
        lax.broadcasted_iota(jnp.int32, (depth, depth), 0)
        == lax.broadcasted_iota(jnp.int32, (depth, depth), 1)
    )
    eye = jnp.where(eye, 1.0, 0.0).astype(jnp.bfloat16)
    owner = lax.broadcasted_iota(jnp.int32, (extra, width), 1) // size
    hot = owner == lax.broadcasted_iota(jnp.int32, (extra, width), 0)
    hot = jnp.where(hot, 1.0, 0.0).astype(jnp.bfloat16)
    for g in range(groups):
        part = wide[:, g * size : (g + 1) * size, :].reshape(width, depth).astype(jnp.bfloat16)
        turned = lax.dot_general(eye, part, CONTRACT_LAST, preferred_element_type=jnp.float32)
        turned_ref[g, :depth, :] = turned.astype(turned_ref.dtype)
        turned_ref[g, depth:, :] = hot
    fetch_key.wait()


def split_keys(key_refs, counts, keys, plain):
    groups = keys.shape[0]
    block = plain.shape[0] // groups

    def split(ref, index, first):
        plain[...] = ref[pl.ds(index * groups * block, groups * block), :].astype(jnp.float32)
        for g in range(groups):
            part = plain[pl.ds(g, block, stride=groups), :]
            keys[g, pl.ds(first, block), :] = part.astype(keys.dtype)

    done = 0
    for ref, count in zip(key_refs, counts, strict=True):
        if count == 1:
            split(ref, 0, done * block)
        else:

            @pl.loop(0, count)
            def _(i, ref=ref, done=done):
                split(ref, i, pl.multiple_of((done + i) * block, block))

        done += count


def tile_of(step, width):
    across = width // LANES
    first = (step % across) * LANES
    return step // across, pl.ds(pl.multiple_of(first, LANES), LANES)


def raw_scores(keys, mask_ref, turned_ref, step, here, base, held, top):
    g, lanes = tile_of(step, turned_ref.shape[2])
    shown = pl.ds(here.start + base, here.size)
    left = jnp.concatenate([keys[g, here, :], mask_ref[shown, :]], axis=1)
    value = lax.dot_general(
        left, turned_ref[g, :, lanes], CONTRACT_INNER, preferred_element_type=jnp.float32
    )
    held[here, :] = value
    return jnp.maximum(top, jnp.max(value.reshape(here.size // 8, 8, LANES), axis=0))


def stage_kernel(base, mask_ref, turned_ref, *refs):
    *key_refs, term_ref, top_ref, sum_ref, keys, plain, even, odd = refs
    amount, depth = keys.shape[1:]
    width = turned_ref.shape[2]
    chunk = math.gcd(amount, CHUNK)
    factor = math.log2(math.e) / math.sqrt(depth)
    split_keys(key_refs, [1] * len(key_refs), keys, plain)
    tiles = keys.shape[0] * (width // LANES)
    tops = {}
    for step in range(tiles + 1):
        top = jnp.full((8, LANES), LOW, jnp.float32)
        summed = jnp.zeros((8, LANES), jnp.float32)
        columns = pl.ds((step - 1) * LANES, LANES)
        for b in range(amount // chunk):
            here = pl.ds(b * chunk, chunk)
            if step:
                held = (even, odd)[(step - 1) % 2]
                value = jnp.exp2((held[here, :] - tops[step - 1]) * factor)
                term_ref[here, columns] = value
                summed = summed + jnp.sum(value.reshape(chunk // 8, 8, LANES), axis=0)
            if step < tiles:
                held = (even, odd)[step % 2]
                top = raw_scores(keys, mask_ref, turned_ref, step, here, base, held, top)
        if step:
            top_ref[:, columns] = tops[step - 1]
            sum_ref[:, columns] = jnp.sum(summed, axis=0, keepdims=True)
        tops[step] = jnp.max(top, axis=0, keepdims=True)


def column_kernel(owners, counts, copies, rows, early, mask_ref, turned_ref, *refs):
    stages = [refs[3 * i : 3 * i + 3] for i in range(early)]
    refs = refs[3 * early :]
    key_refs, (out_ref, keys, plain, total, *scores) = refs[: len(counts)], refs[len(counts) :]
    groups, amount, depth = keys.shape
    width = turned_ref.shape[2]
    block = plain.shape[0] // groups
    chunk = math.gcd(amount, CHUNK)
    factor = math.log2(math.e) / math.sqrt(depth)
    every = total.shape[0]
    base = every - amount
    split_keys(key_refs, counts, keys, plain)
    tiles = groups * (width // LANES)

    def score(step, here, held, top):
        return raw_scores(keys, mask_ref, turned_ref, step, here, base, held, top)

    def term(here, held, top, summed):
        value = jnp.exp2((held[here, :] - top) * factor)
        held[here, :] = value
        return summed + jnp.sum(value.reshape(here.size // 8, 8, LANES), axis=0)

    def spread(value, weight, there, first):
        value = value * weight
        part = value[:, :128]
        for i in range(1, LANES // 128):
            part = part + value[:, i * 128 : (i + 1) * 128]
        total[there, :] = part if first else total[there, :] + part

    lowest = jnp.full((8, LANES), LOW, jnp.float32)
    nothing = jnp.zeros((8, LANES), jnp.float32)
    if amount <= SPAN:
        top, weights = {}, {}
        parts = amount // chunk
        for step in range(tiles + 2):
            high, summed = lowest, nothing
            old = step - 2
            for b in range(parts):
                here = pl.ds(b * chunk, chunk)
                if 0 <= old:
                    first = 0
                    columns = pl.ds(old * LANES, LANES)
                    for (terms, _, _), weight in zip(stages, weights[old][1:], strict=True):
                        size = terms.shape[0] // parts
                        value = terms[pl.ds(b * size, size), columns]
                        spread(value, weight, pl.ds(first + b * size, size), old == 0)
                        first += terms.shape[0]
                    value = scores[old % 3][here, :]
                    spread(value, weights[old][0], pl.ds(base + b * chunk, chunk), old == 0)
                if 0 <= step - 1 < tiles:
                    summed = term(here, scores[(step - 1) % 3], top[step - 1], summed)
                if step < tiles:
                    high = score(step, here, scores[step % 3], high)
            if 0 <= step - 1 < tiles:
                columns = pl.ds((step - 1) * LANES, LANES)
                whole = jnp.sum(summed, axis=0, keepdims=True)
                scale = [jnp.exp2((s[1][:, columns] - top[step - 1]) * factor) for s in stages]
                for s, by in zip(stages, scale, strict=True):
                    whole = whole + s[2][:, columns] * by
                share = 1.0 / whole
                weights[step - 1] = [share] + [share * by for by in scale]
            if step < tiles:
                columns = pl.ds(step * LANES, LANES)
                peak = jnp.max(high, axis=0, keepdims=True)
                for s in stages:
                    peak = jnp.maximum(peak, s[1][:, columns])
                top[step] = peak
    else:
        total[...] = jnp.zeros_like(total)

        def over(body, carry):
            def at(i, c):
                return body(pl.ds(pl.multiple_of(i * chunk, chunk), chunk), c)

            return lax.fori_loop(0, amount // chunk, at, carry)

        @pl.loop(0, tiles)
        def _(step):
            held = scores[0]
            high = over(lambda here, c: score(step, here, held, c), lowest)
            peak = jnp.max(high, axis=0, keepdims=True)
            summed = over(lambda here, c: term(here, held, peak, c), nothing)
            share = 1.0 / jnp.sum(summed, axis=0, keepdims=True)

            def last(here, c):
                spread(held[here, :], share, here, False)
                return c

            over(last, 0)

    ones = jnp.ones((16, 128), jnp.bfloat16)

    def finish(index):
        here = pl.ds(pl.multiple_of(index * block, block), block)
        high = total[here, :].astype(jnp.bfloat16)
        low = (total[here, :] - high.astype(jnp.float32)).astype(jnp.bfloat16)
        line = sum(
            lax.dot_general(ones, part, CONTRACT_LAST, preferred_element_type=jnp.float32)
            for part in (high, low)
        )[:1]
        row = owner_of(index, owners)
        line = line * (1.0 / (width // rows))
        for i in range(copies):
            out_ref[i * (every // block) + row, :, :] = line

    if amount <= SPAN:
        for index in range(every // block):
            finish(index)
    else:
        pl.loop(0, every // block)(finish)


def ring_of(chips):
    return list(range(0, chips, 2)) + list(range(1, chips, 2))[::-1]


def gather_keys(key_vectors):
    size = lax.axis_size("seq")
    ring = ring_of(size // 2)
    place = {chip: i for i, chip in enumerate(ring)}

    def chip_at(chip, steps):
        return ring[(place[chip] + steps) % len(ring)]

    swap = [(i, i ^ 1) for i in range(size)]
    ahead = [(i, 2 * chip_at(i // 2, 1) + i % 2) for i in range(size)]
    blocks = {"own": key_vectors}
    blocks["left"] = lax.ppermute(key_vectors, "seq", ahead)
    blocks["right"] = lax.ppermute(key_vectors, "seq", sorted((j, i) for i, j in ahead))
    blocks["far"] = lax.ppermute(blocks["left"], "seq", ahead)
    found = []
    for block in blocks.values():
        found += [block, lax.ppermute(block, "seq", swap)]
    return found, [[chip_at(i, by) for i in range(size // 2)] for by in (0, -1, 1, -2)]


def on_device(sampled_rows, query_vectors, key_vectors):
    local_rows, heads, depth = query_vectors.shape
    local_keys, groups, _ = key_vectors.shape
    width = local_rows * heads // groups
    members = lax.axis_size("seq")
    others = lax.axis_size("kv")
    amount = members * local_keys
    extra = round_up(local_rows, 128)
    if members == 8:
        blocks, owners = gather_keys(key_vectors)
        early, counts = [2, 2, 2, 1], [1]
    else:
        blocks, owners = [lax.all_gather(key_vectors, "seq", axis=0, tiled=True)], None
        early, counts = [], [members]
    blocks = [b.reshape(-1, depth) for b in blocks]
    mask, turned, own = pl.pallas_call(
        functools.partial(prepare_kernel, members, owners),
        out_shape=(
            jax.ShapeDtypeStruct((amount, extra), jnp.bfloat16),
            jax.ShapeDtypeStruct((groups, depth + extra, width), jnp.bfloat16),
            jax.ShapeDtypeStruct((local_keys * groups, depth), jnp.bfloat16),
        ),
        in_specs=[WHOLE, ANYWHERE, ANYWHERE],
        out_specs=(WHOLE, WHOLE, WHOLE),
        scratch_shapes=[
            pltpu.VMEM(query_vectors.shape, jnp.bfloat16),
            pltpu.SemaphoreType.DMA((2,)),
        ],
        compiler_params=grant(8 if amount <= SPAN else 32),
        name="prepare",
    )(
        sampled_rows,
        pltpu.with_memory_space_constraint(query_vectors, pltpu.HBM),
        pltpu.with_memory_space_constraint(key_vectors.reshape(-1, depth), pltpu.HBM),
    )
    if early:
        blocks[0] = own
    stages = []
    for i, blocks_here in enumerate(early):
        first, some = sum(early[:i]), blocks_here * local_keys
        stages += pl.pallas_call(
            functools.partial(stage_kernel, first * local_keys),
            out_shape=(
                jax.ShapeDtypeStruct((some, groups * width), jnp.float32),
                jax.ShapeDtypeStruct((1, groups * width), jnp.float32),
                jax.ShapeDtypeStruct((1, groups * width), jnp.float32),
            ),
            in_specs=[WHOLE] * (2 + blocks_here),
            out_specs=(WHOLE,) * 3,
            scratch_shapes=[
                pltpu.VMEM((groups, some, depth), jnp.bfloat16),
                pltpu.VMEM((groups * local_keys, depth), jnp.float32),
            ]
            + [pltpu.VMEM((some, LANES), jnp.float32)] * 2,
            compiler_params=grant(12),
        )(mask, turned, *blocks[first : first + blocks_here])
    blocks = blocks[sum(early) :]
    left = sum(counts) * local_keys
    partial = pl.pallas_call(
        functools.partial(column_kernel, owners, counts, others, local_rows, len(early)),
        out_shape=jax.ShapeDtypeStruct((others * members, 1, local_keys), jnp.float32),
        in_specs=[WHOLE] * (2 + len(stages) + len(blocks)),
        out_specs=WHOLE,
        scratch_shapes=[
            pltpu.VMEM((groups, left, depth), jnp.bfloat16),
            pltpu.VMEM((groups * local_keys, depth), jnp.float32),
            pltpu.VMEM((amount, 128), jnp.float32),
        ]
        + [pltpu.VMEM((left, LANES), jnp.float32)] * (3 if left <= SPAN else 1),
        compiler_params=grant(24 if left <= SPAN else 60),
        name="columns",
    )(mask, turned, *stages, *blocks)
    received = lax.all_to_all(partial, ("kv", "seq"), 0, 0, tiled=True)
    return jnp.sum(received, axis=(0, 1))


def solution(mesh):
    placed = (P(), P("seq", "kv", None), P("seq", "kv", None))
    return jax.shard_map(on_device, mesh=mesh, in_specs=placed, out_specs=P("seq"), check_vma=False)
```

```python
import functools
import math

import jax
import jax.numpy as jnp
from jax import lax
from jax.experimental import pallas as pl
from jax.experimental.pallas import tpu as pltpu
from jax.sharding import PartitionSpec as P


NEG = -1e30
LOW = -1e20
SPAN = 2048
LANES = 256
CHUNK = 128
CONTRACT_LAST = (((1,), (1,)), ((), ()))
CONTRACT_INNER = (((1,), (0,)), ((), ()))
WHOLE = pl.BlockSpec(memory_space=pltpu.VMEM)
ANYWHERE = pl.BlockSpec(memory_space=pltpu.HBM)


def grant(mebibytes):
    return pltpu.CompilerParams(vmem_limit_bytes=mebibytes << 20)


def round_up(value, step):
    return -(-value // step) * step


def owner_of(index, owners):
    if owners is None:
        return index
    me = lax.axis_index("seq")
    chip = sum(jnp.where(me // 2 == i, owner, 0) for i, owner in enumerate(owners[index // 2]))
    return 2 * chip + ((me % 2) ^ (index % 2))


def prepare_kernel(members, owners, row_ref, query_hbm, key_hbm, mask_ref, turned_ref, key_ref, query_ref, sem):
    rows, heads, depth = query_ref.shape
    groups, _, width = turned_ref.shape
    fetch_query = pltpu.make_async_copy(query_hbm, query_ref, sem.at[0])
    fetch_key = pltpu.make_async_copy(key_hbm, key_ref, sem.at[1])
    fetch_query.start()
    fetch_key.start()
    size = heads // groups
    extra = mask_ref.shape[1]
    block = mask_ref.shape[0] // members
    column = lax.broadcasted_iota(jnp.int32, (block, extra), 1)
    place = lax.broadcasted_iota(jnp.int32, (block, extra), 0)
    first = lax.axis_index("seq") * rows
    total = row_ref.shape[0]
    back = lax.rem(total - first, total)
    position = pltpu.roll(row_ref[...].reshape(1, total), back, 1)[:, :extra]

    def mask(index):
        hidden = (place + owner_of(index, owners) * block > position) & (column < rows)
        value = jnp.where(hidden, NEG, 0.0)
        here = index * block
        here = here if owners else pl.multiple_of(here, block)
        mask_ref[pl.ds(here, block), :] = value.astype(mask_ref.dtype)

    if owners is None:
        pl.loop(0, members)(mask)
    else:
        for index in range(members):
            mask(index)
    fetch_query.wait()
    wide = query_ref[...].astype(jnp.float32)
    eye = (
        lax.broadcasted_iota(jnp.int32, (depth, depth), 0)
        == lax.broadcasted_iota(jnp.int32, (depth, depth), 1)
    )
    eye = jnp.where(eye, 1.0, 0.0).astype(jnp.bfloat16)
    owner = lax.broadcasted_iota(jnp.int32, (extra, width), 1) // size
    hot = owner == lax.broadcasted_iota(jnp.int32, (extra, width), 0)
    hot = jnp.where(hot, 1.0, 0.0).astype(jnp.bfloat16)
    for g in range(groups):
        part = wide[:, g * size : (g + 1) * size, :].reshape(width, depth).astype(jnp.bfloat16)
        turned = lax.dot_general(eye, part, CONTRACT_LAST, preferred_element_type=jnp.float32)
        turned_ref[g, :depth, :] = turned.astype(turned_ref.dtype)
        turned_ref[g, depth:, :] = hot
    fetch_key.wait()


def split_keys(key_refs, counts, keys, plain):
    groups = keys.shape[0]
    block = plain.shape[0] // groups

    def split(ref, index, first):
        plain[...] = ref[pl.ds(index * groups * block, groups * block), :].astype(jnp.float32)
        for g in range(groups):
            part = plain[pl.ds(g, block, stride=groups), :]
            keys[g, pl.ds(first, block), :] = part.astype(keys.dtype)

    done = 0
    for ref, count in zip(key_refs, counts, strict=True):
        if count == 1:
            split(ref, 0, done * block)
        else:

            @pl.loop(0, count)
            def _(i, ref=ref, done=done):
                split(ref, i, pl.multiple_of((done + i) * block, block))

        done += count


def tile_of(step, width):
    across = width // LANES
    first = (step % across) * LANES
    return step // across, pl.ds(pl.multiple_of(first, LANES), LANES)


def raw_scores(keys, mask_ref, turned_ref, step, here, base, held, top):
    g, lanes = tile_of(step, turned_ref.shape[2])
    shown = pl.ds(here.start + base, here.size)
    left = jnp.concatenate([keys[g, here, :], mask_ref[shown, :]], axis=1)
    value = lax.dot_general(
        left, turned_ref[g, :, lanes], CONTRACT_INNER, preferred_element_type=jnp.float32
    )
    held[here, :] = value
    return jnp.maximum(top, jnp.max(value.reshape(here.size // 8, 8, LANES), axis=0))


def stage_kernel(base, mask_ref, turned_ref, *refs):
    *key_refs, term_ref, top_ref, sum_ref, keys, plain, even, odd = refs
    amount, depth = keys.shape[1:]
    width = turned_ref.shape[2]
    chunk = math.gcd(amount, CHUNK)
    factor = math.log2(math.e) / math.sqrt(depth)
    split_keys(key_refs, [1] * len(key_refs), keys, plain)
    tiles = keys.shape[0] * (width // LANES)
    tops = {}
    for step in range(tiles + 1):
        top = jnp.full((8, LANES), LOW, jnp.float32)
        summed = jnp.zeros((8, LANES), jnp.float32)
        columns = pl.ds((step - 1) * LANES, LANES)
        for b in range(amount // chunk):
            here = pl.ds(b * chunk, chunk)
            if step:
                held = (even, odd)[(step - 1) % 2]
                value = jnp.exp2((held[here, :] - tops[step - 1]) * factor)
                term_ref[here, columns] = value
                summed = summed + jnp.sum(value.reshape(chunk // 8, 8, LANES), axis=0)
            if step < tiles:
                held = (even, odd)[step % 2]
                top = raw_scores(keys, mask_ref, turned_ref, step, here, base, held, top)
        if step:
            top_ref[:, columns] = tops[step - 1]
            sum_ref[:, columns] = jnp.sum(summed, axis=0, keepdims=True)
        tops[step] = jnp.max(top, axis=0, keepdims=True)


def column_kernel(owners, counts, copies, rows, early, mask_ref, turned_ref, *refs):
    stages = [refs[3 * i : 3 * i + 3] for i in range(early)]
    refs = refs[3 * early :]
    key_refs, (out_ref, keys, plain, total, *scores) = refs[: len(counts)], refs[len(counts) :]
    groups, amount, depth = keys.shape
    width = turned_ref.shape[2]
    block = plain.shape[0] // groups
    chunk = math.gcd(amount, CHUNK)
    factor = math.log2(math.e) / math.sqrt(depth)
    every = total.shape[0]
    base = every - amount
    split_keys(key_refs, counts, keys, plain)
    tiles = groups * (width // LANES)

    def score(step, here, held, top):
        return raw_scores(keys, mask_ref, turned_ref, step, here, base, held, top)

    def term(here, held, top, summed):
        value = jnp.exp2((held[here, :] - top) * factor)
        held[here, :] = value
        return summed + jnp.sum(value.reshape(here.size // 8, 8, LANES), axis=0)

    def spread(value, weight, there, first):
        value = value * weight
        part = value[:, :128]
        for i in range(1, LANES // 128):
            part = part + value[:, i * 128 : (i + 1) * 128]
        total[there, :] = part if first else total[there, :] + part

    lowest = jnp.full((8, LANES), LOW, jnp.float32)
    nothing = jnp.zeros((8, LANES), jnp.float32)
    if amount <= SPAN:
        top, weights = {}, {}
        parts = amount // chunk
        for step in range(tiles + 2):
            high, summed = lowest, nothing
            old = step - 2
            for b in range(parts):
                here = pl.ds(b * chunk, chunk)
                if 0 <= old:
                    first = 0
                    columns = pl.ds(old * LANES, LANES)
                    for (terms, _, _), weight in zip(stages, weights[old][1:], strict=True):
                        size = terms.shape[0] // parts
                        value = terms[pl.ds(b * size, size), columns]
                        spread(value, weight, pl.ds(first + b * size, size), old == 0)
                        first += terms.shape[0]
                    value = scores[old % 3][here, :]
                    spread(value, weights[old][0], pl.ds(base + b * chunk, chunk), old == 0)
                if 0 <= step - 1 < tiles:
                    summed = term(here, scores[(step - 1) % 3], top[step - 1], summed)
                if step < tiles:
                    high = score(step, here, scores[step % 3], high)
            if 0 <= step - 1 < tiles:
                columns = pl.ds((step - 1) * LANES, LANES)
                whole = jnp.sum(summed, axis=0, keepdims=True)
                scale = [jnp.exp2((s[1][:, columns] - top[step - 1]) * factor) for s in stages]
                for s, by in zip(stages, scale, strict=True):
                    whole = whole + s[2][:, columns] * by
                share = 1.0 / whole
                weights[step - 1] = [share] + [share * by for by in scale]
            if step < tiles:
                columns = pl.ds(step * LANES, LANES)
                peak = jnp.max(high, axis=0, keepdims=True)
                for s in stages:
                    peak = jnp.maximum(peak, s[1][:, columns])
                top[step] = peak
    else:
        total[...] = jnp.zeros_like(total)

        def over(body, carry):
            def at(i, c):
                return body(pl.ds(pl.multiple_of(i * chunk, chunk), chunk), c)

            return lax.fori_loop(0, amount // chunk, at, carry)

        @pl.loop(0, tiles)
        def _(step):
            held = scores[0]
            high = over(lambda here, c: score(step, here, held, c), lowest)
            peak = jnp.max(high, axis=0, keepdims=True)
            summed = over(lambda here, c: term(here, held, peak, c), nothing)
            share = 1.0 / jnp.sum(summed, axis=0, keepdims=True)

            def last(here, c):
                spread(held[here, :], share, here, False)
                return c

            over(last, 0)

    ones = jnp.ones((16, 128), jnp.bfloat16)

    def finish(index):
        here = pl.ds(pl.multiple_of(index * block, block), block)
        high = total[here, :].astype(jnp.bfloat16)
        low = (total[here, :] - high.astype(jnp.float32)).astype(jnp.bfloat16)
        line = sum(
            lax.dot_general(ones, part, CONTRACT_LAST, preferred_element_type=jnp.float32)
            for part in (high, low)
        )[:1]
        row = owner_of(index, owners)
        line = line * (1.0 / (width // rows))
        for i in range(copies):
            out_ref[i * (every // block) + row, :, :] = line

    if amount <= SPAN:
        for index in range(every // block):
            finish(index)
    else:
        pl.loop(0, every // block)(finish)


def ring_of(chips):
    return list(range(0, chips, 2)) + list(range(1, chips, 2))[::-1]


def pick_kernel(ends, near_ref, far_ref, out_ref):
    chip = lax.axis_index("seq") // 2
    outer = (chip == ends[0]) | (chip == ends[1])

    @pl.when(outer)
    def _():
        out_ref[...] = far_ref[...]

    @pl.when(jnp.logical_not(outer))
    def _():
        out_ref[...] = near_ref[...]


def gather_keys(key_vectors):
    size = lax.axis_size("seq")
    ring = ring_of(size // 2)
    place = {chip: i for i, chip in enumerate(ring)}

    def chip_at(chip, steps):
        return ring[(place[chip] + steps) % len(ring)]

    swap = [(i, i ^ 1) for i in range(size)]
    ahead = [(i, 2 * chip_at(i // 2, 1) + i % 2) for i in range(size)]
    blocks = {"own": key_vectors}
    blocks["left"] = lax.ppermute(key_vectors, "seq", ahead)
    blocks["right"] = lax.ppermute(key_vectors, "seq", sorted((j, i) for i, j in ahead))
    ends = (0, size // 2 - 1)
    beside = [(i, i ^ 1 if i // 2 in ends else i ^ 6) for i in range(size)]
    near = lax.ppermute(key_vectors, "seq", beside)
    far = lax.ppermute(blocks["left"], "seq", [(i, i ^ 2) for i in range(size)])
    flat = [b.reshape(-1, b.shape[-1]) for b in (near, far)]
    blocks["far"] = pl.pallas_call(
        functools.partial(pick_kernel, ends),
        out_shape=jax.ShapeDtypeStruct(flat[0].shape, near.dtype),
        in_specs=[WHOLE] * 2,
        out_specs=WHOLE,
        compiler_params=grant(2),
        name="pick",
    )(*flat).reshape(near.shape)
    found = []
    for block in blocks.values():
        found += [block, lax.ppermute(block, "seq", swap)]
    return found, [[chip_at(i, by) for i in range(size // 2)] for by in (0, -1, 1, -2)]


def on_device(sampled_rows, query_vectors, key_vectors):
    local_rows, heads, depth = query_vectors.shape
    local_keys, groups, _ = key_vectors.shape
    width = local_rows * heads // groups
    members = lax.axis_size("seq")
    others = lax.axis_size("kv")
    amount = members * local_keys
    extra = round_up(local_rows, 128)
    if members == 8:
        blocks, owners = gather_keys(key_vectors)
        early, counts = [2, 2, 2, 1], [1]
    else:
        blocks, owners = [lax.all_gather(key_vectors, "seq", axis=0, tiled=True)], None
        early, counts = [], [members]
    blocks = [b.reshape(-1, depth) for b in blocks]
    mask, turned, own = pl.pallas_call(
        functools.partial(prepare_kernel, members, owners),
        out_shape=(
            jax.ShapeDtypeStruct((amount, extra), jnp.bfloat16),
            jax.ShapeDtypeStruct((groups, depth + extra, width), jnp.bfloat16),
            jax.ShapeDtypeStruct((local_keys * groups, depth), jnp.bfloat16),
        ),
        in_specs=[WHOLE, ANYWHERE, ANYWHERE],
        out_specs=(WHOLE, WHOLE, WHOLE),
        scratch_shapes=[
            pltpu.VMEM(query_vectors.shape, jnp.bfloat16),
            pltpu.SemaphoreType.DMA((2,)),
        ],
        compiler_params=grant(8 if amount <= SPAN else 32),
        name="prepare",
    )(
        sampled_rows,
        pltpu.with_memory_space_constraint(query_vectors, pltpu.HBM),
        pltpu.with_memory_space_constraint(key_vectors.reshape(-1, depth), pltpu.HBM),
    )
    if early:
        blocks[0] = own
    stages = []
    for i, blocks_here in enumerate(early):
        first, some = sum(early[:i]), blocks_here * local_keys
        stages += pl.pallas_call(
            functools.partial(stage_kernel, first * local_keys),
            out_shape=(
                jax.ShapeDtypeStruct((some, groups * width), jnp.float32),
                jax.ShapeDtypeStruct((1, groups * width), jnp.float32),
                jax.ShapeDtypeStruct((1, groups * width), jnp.float32),
            ),
            in_specs=[WHOLE] * (2 + blocks_here),
            out_specs=(WHOLE,) * 3,
            scratch_shapes=[
                pltpu.VMEM((groups, some, depth), jnp.bfloat16),
                pltpu.VMEM((groups * local_keys, depth), jnp.float32),
            ]
            + [pltpu.VMEM((some, LANES), jnp.float32)] * 2,
            compiler_params=grant(8),
        )(mask, turned, *blocks[first : first + blocks_here])
    blocks = blocks[sum(early) :]
    left = sum(counts) * local_keys
    partial = pl.pallas_call(
        functools.partial(column_kernel, owners, counts, others, local_rows, len(early)),
        out_shape=jax.ShapeDtypeStruct((others * members, 1, local_keys), jnp.float32),
        in_specs=[WHOLE] * (2 + len(stages) + len(blocks)),
        out_specs=WHOLE,
        scratch_shapes=[
            pltpu.VMEM((groups, left, depth), jnp.bfloat16),
            pltpu.VMEM((groups * local_keys, depth), jnp.float32),
            pltpu.VMEM((amount, 128), jnp.float32),
        ]
        + [pltpu.VMEM((left, LANES), jnp.float32)] * (3 if left <= SPAN else 1),
        compiler_params=grant(10 if left <= SPAN else 60),
        name="columns",
    )(mask, turned, *stages, *blocks)
    received = lax.all_to_all(partial, ("kv", "seq"), 0, 0, tiled=True)
    return jnp.sum(received, axis=(0, 1))


def solution(mesh):
    placed = (P(), P("seq", "kv", None), P("seq", "kv", None))
    return jax.shard_map(on_device, mesh=mesh, in_specs=placed, out_specs=P("seq"), check_vma=False)
```

```python
import functools
import math

import jax
import jax.numpy as jnp
from jax import lax
from jax.experimental import pallas as pl
from jax.experimental.pallas import tpu as pltpu
from jax.sharding import PartitionSpec as P


NEG = -1e30
LOW = -1e20
SPAN = 2048
LANES = 256
CHUNK = 128
CONTRACT_LAST = (((1,), (1,)), ((), ()))
CONTRACT_INNER = (((1,), (0,)), ((), ()))
WHOLE = pl.BlockSpec(memory_space=pltpu.VMEM)
ANYWHERE = pl.BlockSpec(memory_space=pltpu.HBM)


def grant(mebibytes):
    return pltpu.CompilerParams(vmem_limit_bytes=mebibytes << 20)


def round_up(value, step):
    return -(-value // step) * step


def owner_of(index, owners):
    if owners is None:
        return index
    me = lax.axis_index("seq")
    chip = sum(jnp.where(me // 2 == i, owner, 0) for i, owner in enumerate(owners[index // 2]))
    return 2 * chip + ((me % 2) ^ (index % 2))


def prepare_kernel(members, owners, row_ref, query_hbm, key_hbm, mask_ref, turned_ref, key_ref, query_ref, sem):
    rows, heads, depth = query_ref.shape
    groups, _, width = turned_ref.shape
    fetch_query = pltpu.make_async_copy(query_hbm, query_ref, sem.at[0])
    fetch_key = pltpu.make_async_copy(key_hbm, key_ref, sem.at[1])
    fetch_query.start()
    fetch_key.start()
    size = heads // groups
    extra = mask_ref.shape[1]
    block = mask_ref.shape[0] // members
    column = lax.broadcasted_iota(jnp.int32, (block, extra), 1)
    place = lax.broadcasted_iota(jnp.int32, (block, extra), 0)
    first = lax.axis_index("seq") * rows
    total = row_ref.shape[0]
    back = lax.rem(total - first, total)
    position = pltpu.roll(row_ref[...].reshape(1, total), back, 1)[:, :extra]

    def mask(index):
        hidden = (place + owner_of(index, owners) * block > position) & (column < rows)
        value = jnp.where(hidden, NEG, 0.0)
        here = index * block
        here = here if owners else pl.multiple_of(here, block)
        mask_ref[pl.ds(here, block), :] = value.astype(mask_ref.dtype)

    if owners is None:
        pl.loop(0, members)(mask)
    else:
        for index in range(members):
            mask(index)
    fetch_query.wait()
    wide = query_ref[...].astype(jnp.float32)
    eye = (
        lax.broadcasted_iota(jnp.int32, (depth, depth), 0)
        == lax.broadcasted_iota(jnp.int32, (depth, depth), 1)
    )
    eye = jnp.where(eye, 1.0, 0.0).astype(jnp.bfloat16)
    owner = lax.broadcasted_iota(jnp.int32, (extra, width), 1) // size
    hot = owner == lax.broadcasted_iota(jnp.int32, (extra, width), 0)
    hot = jnp.where(hot, 1.0, 0.0).astype(jnp.bfloat16)
    for g in range(groups):
        part = wide[:, g * size : (g + 1) * size, :].reshape(width, depth).astype(jnp.bfloat16)
        turned = lax.dot_general(eye, part, CONTRACT_LAST, preferred_element_type=jnp.float32)
        turned_ref[g, :depth, :] = turned.astype(turned_ref.dtype)
        turned_ref[g, depth:, :] = hot
    fetch_key.wait()


def split_keys(key_refs, counts, keys, plain):
    groups = keys.shape[0]
    block = plain.shape[0] // groups

    def split(ref, index, first):
        plain[...] = ref[pl.ds(index * groups * block, groups * block), :].astype(jnp.float32)
        for g in range(groups):
            part = plain[pl.ds(g, block, stride=groups), :]
            keys[g, pl.ds(first, block), :] = part.astype(keys.dtype)

    done = 0
    for ref, count in zip(key_refs, counts, strict=True):
        if count == 1:
            split(ref, 0, done * block)
        else:

            @pl.loop(0, count)
            def _(i, ref=ref, done=done):
                split(ref, i, pl.multiple_of((done + i) * block, block))

        done += count


def tile_of(step, width):
    across = width // LANES
    first = (step % across) * LANES
    return step // across, pl.ds(pl.multiple_of(first, LANES), LANES)


def raw_scores(keys, mask_ref, turned_ref, step, here, base, held, top):
    g, lanes = tile_of(step, turned_ref.shape[2])
    shown = pl.ds(here.start + base, here.size)
    left = jnp.concatenate([keys[g, here, :], mask_ref[shown, :]], axis=1)
    value = lax.dot_general(
        left, turned_ref[g, :, lanes], CONTRACT_INNER, preferred_element_type=jnp.float32
    )
    held[here, :] = value
    return jnp.maximum(top, jnp.max(value.reshape(here.size // 8, 8, LANES), axis=0))


def stage_kernel(base, mask_ref, turned_ref, *refs):
    *key_refs, term_ref, top_ref, sum_ref, keys, plain, even, odd = refs
    amount, depth = keys.shape[1:]
    width = turned_ref.shape[2]
    chunk = math.gcd(amount, CHUNK)
    factor = math.log2(math.e) / math.sqrt(depth)
    split_keys(key_refs, [1] * len(key_refs), keys, plain)
    tiles = keys.shape[0] * (width // LANES)
    tops = {}
    for step in range(tiles + 1):
        top = jnp.full((8, LANES), LOW, jnp.float32)
        summed = jnp.zeros((8, LANES), jnp.float32)
        columns = pl.ds((step - 1) * LANES, LANES)
        for b in range(amount // chunk):
            here = pl.ds(b * chunk, chunk)
            if step:
                held = (even, odd)[(step - 1) % 2]
                value = jnp.exp2((held[here, :] - tops[step - 1]) * factor)
                term_ref[here, columns] = value
                summed = summed + jnp.sum(value.reshape(chunk // 8, 8, LANES), axis=0)
            if step < tiles:
                held = (even, odd)[step % 2]
                top = raw_scores(keys, mask_ref, turned_ref, step, here, base, held, top)
        if step:
            top_ref[:, columns] = tops[step - 1]
            sum_ref[:, columns] = jnp.sum(summed, axis=0, keepdims=True)
        tops[step] = jnp.max(top, axis=0, keepdims=True)


def column_kernel(owners, counts, copies, rows, early, mask_ref, turned_ref, *refs):
    stages = [refs[3 * i : 3 * i + 3] for i in range(early)]
    refs = refs[3 * early :]
    key_refs, (out_ref, keys, plain, total, *scores) = refs[: len(counts)], refs[len(counts) :]
    groups, amount, depth = keys.shape
    width = turned_ref.shape[2]
    block = plain.shape[0] // groups
    chunk = math.gcd(amount, CHUNK)
    factor = math.log2(math.e) / math.sqrt(depth)
    every = total.shape[0]
    base = every - amount
    split_keys(key_refs, counts, keys, plain)
    tiles = groups * (width // LANES)

    def score(step, here, held, top):
        return raw_scores(keys, mask_ref, turned_ref, step, here, base, held, top)

    def term(here, held, top, summed):
        value = jnp.exp2((held[here, :] - top) * factor)
        held[here, :] = value
        return summed + jnp.sum(value.reshape(here.size // 8, 8, LANES), axis=0)

    def spread(value, weight, there, first):
        value = value * weight
        part = value[:, :128]
        for i in range(1, LANES // 128):
            part = part + value[:, i * 128 : (i + 1) * 128]
        total[there, :] = part if first else total[there, :] + part

    lowest = jnp.full((8, LANES), LOW, jnp.float32)
    nothing = jnp.zeros((8, LANES), jnp.float32)
    if amount <= SPAN:
        top, weights = {}, {}
        parts = amount // chunk
        for step in range(tiles + 2):
            high, summed = lowest, nothing
            old = step - 2
            for b in range(parts):
                here = pl.ds(b * chunk, chunk)
                if 0 <= old:
                    first = 0
                    columns = pl.ds(old * LANES, LANES)
                    for (terms, _, _), weight in zip(stages, weights[old][1:], strict=True):
                        size = terms.shape[0] // parts
                        value = terms[pl.ds(b * size, size), columns]
                        spread(value, weight, pl.ds(first + b * size, size), old == 0)
                        first += terms.shape[0]
                    value = scores[old % 3][here, :]
                    spread(value, weights[old][0], pl.ds(base + b * chunk, chunk), old == 0)
                if 0 <= step - 1 < tiles:
                    summed = term(here, scores[(step - 1) % 3], top[step - 1], summed)
                if step < tiles:
                    high = score(step, here, scores[step % 3], high)
            if 0 <= step - 1 < tiles:
                columns = pl.ds((step - 1) * LANES, LANES)
                whole = jnp.sum(summed, axis=0, keepdims=True)
                scale = [jnp.exp2((s[1][:, columns] - top[step - 1]) * factor) for s in stages]
                for s, by in zip(stages, scale, strict=True):
                    whole = whole + s[2][:, columns] * by
                share = 1.0 / whole
                weights[step - 1] = [share] + [share * by for by in scale]
            if step < tiles:
                columns = pl.ds(step * LANES, LANES)
                peak = jnp.max(high, axis=0, keepdims=True)
                for s in stages:
                    peak = jnp.maximum(peak, s[1][:, columns])
                top[step] = peak
    else:
        total[...] = jnp.zeros_like(total)

        def over(body, carry):
            def at(i, c):
                return body(pl.ds(pl.multiple_of(i * chunk, chunk), chunk), c)

            return lax.fori_loop(0, amount // chunk, at, carry)

        @pl.loop(0, tiles)
        def _(step):
            held = scores[0]
            high = over(lambda here, c: score(step, here, held, c), lowest)
            peak = jnp.max(high, axis=0, keepdims=True)
            summed = over(lambda here, c: term(here, held, peak, c), nothing)
            share = 1.0 / jnp.sum(summed, axis=0, keepdims=True)

            def last(here, c):
                spread(held[here, :], share, here, False)
                return c

            over(last, 0)

    ones = jnp.ones((16, 128), jnp.bfloat16)

    def finish(index):
        here = pl.ds(pl.multiple_of(index * block, block), block)
        high = total[here, :].astype(jnp.bfloat16)
        low = (total[here, :] - high.astype(jnp.float32)).astype(jnp.bfloat16)
        line = sum(
            lax.dot_general(ones, part, CONTRACT_LAST, preferred_element_type=jnp.float32)
            for part in (high, low)
        )[:1]
        row = owner_of(index, owners)
        line = line * (1.0 / (width // rows))
        for i in range(copies):
            out_ref[i * (every // block) + row, :, :] = line

    if amount <= SPAN:
        for index in range(every // block):
            finish(index)
    else:
        pl.loop(0, every // block)(finish)


def ring_of(chips):
    return list(range(0, chips, 2)) + list(range(1, chips, 2))[::-1]


def add_kernel(received_ref, out_ref):
    out_ref[...] = jnp.sum(received_ref[...], axis=(0, 1))


def pick_kernel(ends, near_ref, far_ref, out_ref):
    chip = lax.axis_index("seq") // 2
    outer = (chip == ends[0]) | (chip == ends[1])

    @pl.when(outer)
    def _():
        out_ref[...] = far_ref[...]

    @pl.when(jnp.logical_not(outer))
    def _():
        out_ref[...] = near_ref[...]


def gather_keys(key_vectors):
    size = lax.axis_size("seq")
    ring = ring_of(size // 2)
    place = {chip: i for i, chip in enumerate(ring)}

    def chip_at(chip, steps):
        return ring[(place[chip] + steps) % len(ring)]

    swap = [(i, i ^ 1) for i in range(size)]
    ahead = [(i, 2 * chip_at(i // 2, 1) + i % 2) for i in range(size)]
    blocks = {"own": key_vectors}
    blocks["left"] = lax.ppermute(key_vectors, "seq", ahead)
    blocks["right"] = lax.ppermute(key_vectors, "seq", sorted((j, i) for i, j in ahead))
    ends = (0, size // 2 - 1)
    beside = [(i, i ^ 1 if i // 2 in ends else i ^ 6) for i in range(size)]
    near = lax.ppermute(key_vectors, "seq", beside)
    far = lax.ppermute(blocks["left"], "seq", [(i, i ^ 2) for i in range(size)])
    flat = [b.reshape(-1, b.shape[-1]) for b in (near, far)]
    blocks["far"] = pl.pallas_call(
        functools.partial(pick_kernel, ends),
        out_shape=jax.ShapeDtypeStruct(flat[0].shape, near.dtype),
        in_specs=[WHOLE] * 2,
        out_specs=WHOLE,
        compiler_params=grant(2),
        name="pick",
    )(*flat).reshape(near.shape)
    found = []
    for block in blocks.values():
        found += [block, lax.ppermute(block, "seq", swap)]
    return found, [[chip_at(i, by) for i in range(size // 2)] for by in (0, -1, 1, -2)]


def on_device(sampled_rows, query_vectors, key_vectors):
    local_rows, heads, depth = query_vectors.shape
    local_keys, groups, _ = key_vectors.shape
    width = local_rows * heads // groups
    members = lax.axis_size("seq")
    others = lax.axis_size("kv")
    amount = members * local_keys
    extra = round_up(local_rows, 128)
    if members == 8:
        blocks, owners = gather_keys(key_vectors)
        early, counts = [2, 2, 2, 1], [1]
    else:
        blocks, owners = [lax.all_gather(key_vectors, "seq", axis=0, tiled=True)], None
        early, counts = [], [members]
    blocks = [b.reshape(-1, depth) for b in blocks]
    mask, turned, own = pl.pallas_call(
        functools.partial(prepare_kernel, members, owners),
        out_shape=(
            jax.ShapeDtypeStruct((amount, extra), jnp.bfloat16),
            jax.ShapeDtypeStruct((groups, depth + extra, width), jnp.bfloat16),
            jax.ShapeDtypeStruct((local_keys * groups, depth), jnp.bfloat16),
        ),
        in_specs=[WHOLE, ANYWHERE, ANYWHERE],
        out_specs=(WHOLE, WHOLE, WHOLE),
        scratch_shapes=[
            pltpu.VMEM(query_vectors.shape, jnp.bfloat16),
            pltpu.SemaphoreType.DMA((2,)),
        ],
        compiler_params=grant(8 if amount <= SPAN else 32),
        name="prepare",
    )(
        sampled_rows,
        pltpu.with_memory_space_constraint(query_vectors, pltpu.HBM),
        pltpu.with_memory_space_constraint(key_vectors.reshape(-1, depth), pltpu.HBM),
    )
    if early:
        blocks[0] = own
    stages = []
    for i, blocks_here in enumerate(early):
        first, some = sum(early[:i]), blocks_here * local_keys
        stages += pl.pallas_call(
            functools.partial(stage_kernel, first * local_keys),
            out_shape=(
                jax.ShapeDtypeStruct((some, groups * width), jnp.float32),
                jax.ShapeDtypeStruct((1, groups * width), jnp.float32),
                jax.ShapeDtypeStruct((1, groups * width), jnp.float32),
            ),
            in_specs=[WHOLE] * (2 + blocks_here),
            out_specs=(WHOLE,) * 3,
            scratch_shapes=[
                pltpu.VMEM((groups, some, depth), jnp.bfloat16),
                pltpu.VMEM((groups * local_keys, depth), jnp.float32),
            ]
            + [pltpu.VMEM((some, LANES), jnp.float32)] * 2,
            compiler_params=grant(8),
        )(mask, turned, *blocks[first : first + blocks_here])
    blocks = blocks[sum(early) :]
    left = sum(counts) * local_keys
    partial = pl.pallas_call(
        functools.partial(column_kernel, owners, counts, others, local_rows, len(early)),
        out_shape=jax.ShapeDtypeStruct((others * members, 1, local_keys), jnp.float32),
        in_specs=[WHOLE] * (2 + len(stages) + len(blocks)),
        out_specs=WHOLE,
        scratch_shapes=[
            pltpu.VMEM((groups, left, depth), jnp.bfloat16),
            pltpu.VMEM((groups * local_keys, depth), jnp.float32),
            pltpu.VMEM((amount, 128), jnp.float32),
        ]
        + [pltpu.VMEM((left, LANES), jnp.float32)] * (3 if left <= SPAN else 1),
        compiler_params=grant(10 if left <= SPAN else 60),
        name="columns",
    )(mask, turned, *stages, *blocks)
    received = lax.all_to_all(partial, ("kv", "seq"), 0, 0, tiled=True)
    return pl.pallas_call(
        add_kernel,
        out_shape=jax.ShapeDtypeStruct((local_keys,), jnp.float32),
        in_specs=[WHOLE],
        out_specs=WHOLE,
        compiler_params=grant(4 if amount <= SPAN else 32),
        name="add",
    )(received)


def solution(mesh):
    placed = (P(), P("seq", "kv", None), P("seq", "kv", None))
    return jax.shard_map(on_device, mesh=mesh, in_specs=placed, out_specs=P("seq"), check_vma=False)
```
